128 devices in a mesh: arc: 8 (over z, core), tm: 16 (over y, x).
Axes of the slice: x: 4, y: 4, z: 4, core: 2. Of those that a mesh axis runs over, the one named last changes fastest.
Arguments:
- transition: float32 [8, 6, 6, 512], P('arc', None, None, 'tm'), may hold values from -0.21 to 1.01
- forcing: bfloat16 [8, 512, 6, 9216], P('arc', 'tm'), may hold values from -0.25 to 0.25
- partials: float32 [8, 6, 512], P('arc', None, 'tm'), may hold values from -6 to 6
- observed: float32 [8, 512], P('arc', 'tm'), may hold values from -6 to 6
- counts: int32 [8, 16], P('arc', 'tm'), may hold values from 8 to 32, as said below
Outputs:
- gram: float32 [9216, 1152], P(('arc', 'tm'))
- rhs: float32 [9216], P(('arc', 'tm'))
The draws below stay inside these ranges and needn't reach their ends.
Inputs may be any that keep to these rules, and one draw needn't show every extreme that they name: Shard (a, t) has its first counts[a, t] epochs active; in every draw some shard has all 32 active.
All inputs are finite; a program needn't handle non-finite values.
Results may differ from the reference program's by a relative error of at most 0.013.
Values may be sent and summed in bfloat16 or wider, within the bound.
No kernel may reach another device: no remote copies, remote signals or barrier semaphores. Data moves between devices by JAX's collectives and lax.ppermute only.
A program may use at most 128 MiB of HBM per device.

```python
import jax
import jax.numpy as jnp
from jax import lax

COEFFS = 9216
STATE = 6
EPOCH_DEV = 32
ARCS = 8
TSHARDS = 16
EPOCHS = 512
BLOCK = 1152


def draw_transition(key, part):
    normal_one = jnp.clip(jax.random.normal(jax.random.fold_in(key, 11), (ARCS, 6, 6, EPOCHS), jnp.float32), -4.0, 4.0)
    normal_two = jnp.clip(jax.random.normal(jax.random.fold_in(key, 12), (ARCS, 6, 6, EPOCHS), jnp.float32), -4.0, 4.0)
    twisted = 0.025 * (normal_one - jnp.swapaxes(normal_one, 1, 2))
    identity = jnp.eye(6, dtype=jnp.float32)[None, :, :, None]
    return 0.9969 * identity + twisted + 0.001 * normal_two


def draw_counts(key, part):
    baseline = jax.random.randint(jax.random.fold_in(key, 21), (ARCS * TSHARDS,), EPOCH_DEV // 4, EPOCH_DEV + 1)
    chosen_cell = jax.random.randint(jax.random.fold_in(key, 22), (), 0, ARCS * TSHARDS)
    merged = jnp.where(jnp.arange(ARCS * TSHARDS) == chosen_cell, EPOCH_DEV, baseline)
    return merged.reshape(ARCS, TSHARDS).astype(jnp.int32)


def block_levels(key, dims, shards, low, top_value):
    factor_of, own = 1.0, jax.random.fold_in(key, 6)
    for axis_at, shards_of in shards:
        steps = jnp.exp(jax.random.uniform(jax.random.fold_in(own, axis_at), (shards_of,), jnp.float32, low / len(shards), top_value / len(shards)))
        factor_of = factor_of * jnp.repeat(steps, dims[axis_at] // shards_of).reshape([-1 if axis == axis_at else 1 for axis in range(len(dims))])
    return factor_of


def normal_values(own_key, shape, deviation, reach, split=(), kind=jnp.bfloat16):
    values = deviation * jax.random.normal(own_key, shape, jnp.float32)
    if split:
        values = values * block_levels(own_key, shape, split, -0.22, 0.18)
    return jnp.clip(values, -reach, reach).astype(kind)


def setup_inputs(seed: int = 0) -> dict:
    arg_keys = jax.random.split(jax.random.key(seed), 6)
    return {
        "transition": draw_transition(jax.random.fold_in(arg_keys[5], 71), 0),
        "forcing": normal_values(arg_keys[1], (ARCS, EPOCHS, STATE, COEFFS), EPOCHS ** -0.5, 0.25, ((0, 8), (1, 16))),
        "partials": normal_values(arg_keys[2], (ARCS, STATE, EPOCHS), 1.0, 6.0, ((0, 8), (2, 16)), jnp.float32),
        "observed": normal_values(arg_keys[3], (ARCS, EPOCHS), 1.0, 6.0, ((0, 8), (1, 16)), jnp.float32),
        "counts": draw_counts(jax.random.fold_in(arg_keys[5], 71), 0),
    }


exact_precision = lax.Precision.HIGHEST

def sensitivity_rows(transition, partials):
    epochs = transition.shape[2]
    rows_total = epochs + 6
    columns = epochs + 1
    identity = jnp.eye(6, dtype=jnp.float32)
    head_rows = jnp.concatenate([partials, identity], axis=1)
    row_index = lax.broadcasted_iota(jnp.int32, (rows_total, columns), 0)
    column_index = lax.broadcasted_iota(jnp.int32, (rows_total, columns), 1) - 1
    row_limit = jnp.minimum(row_index, epochs)
    inside = column_index < row_index
    factors = jnp.where(inside, row_limit - 1 - column_index, 0)
    vectors = jnp.where(inside[None, :, :], head_rows[:, :, None], jnp.float32(0.0))
    highest = row_limit - 1
    products = transition
    stride = 1
    for bit_number in range(epochs.bit_length()):
        chosen = factors // stride % 2 == 1
        lowest = jnp.clip(highest - stride + 1, 0, epochs - 1)
        picked = jnp.take(products, lowest, axis=2)
        advanced = jnp.einsum('akl,abkl->bkl', vectors, picked, precision=exact_precision)
        vectors = jnp.where(chosen[None, :, :], advanced, vectors)
        highest = jnp.where(chosen, highest - stride, highest)
        filler = jnp.broadcast_to(identity[:, :, None], (6, 6, min(stride, epochs)))
        shifted = jnp.concatenate([products[:, :, stride:], filler], axis=2)
        products = jnp.einsum('abs,bcs->acs', shifted, products, precision=exact_precision)
        stride = stride * 2
    return vectors

def local_terms(transition, forcing, partials):
    epochs = transition.shape[2]
    vectors = sensitivity_rows(transition, partials)
    to_entry = vectors[:, :, 0]
    weights = jnp.transpose(vectors[:, :, 1:], (1, 2, 0)).reshape(epochs + 6, epochs * 6).astype(jnp.bfloat16)
    flat_forcing = forcing.reshape(epochs * 6, forcing.shape[-1])
    local_sum = jnp.dot(weights.astype(jnp.float32), flat_forcing.astype(jnp.float32), precision=exact_precision)
    return (to_entry, local_sum)

def solve_small(matrix, right):
    factor = jnp.linalg.cholesky(matrix)
    halfway = lax.linalg.triangular_solve(factor, right, left_side=True, lower=True)
    return lax.linalg.triangular_solve(factor, halfway, left_side=True, lower=True, transpose_a=True)

def reference(transition, forcing, partials, observed, counts):
    shard_ids = jnp.arange(ARCS * TSHARDS, dtype=jnp.int32)

    def one_shard(shard_id):
        arc_id = shard_id // TSHARDS
        time_id = shard_id % TSHARDS
        start = (time_id * EPOCH_DEV).astype(jnp.int32)
        trans_shard = lax.dynamic_slice_in_dim(lax.dynamic_index_in_dim(transition, arc_id, 0, False), start, EPOCH_DEV, 2)
        forcing_shard = lax.dynamic_slice_in_dim(lax.dynamic_index_in_dim(forcing, arc_id, 0, False), start, EPOCH_DEV, 0)
        partial_shard = lax.dynamic_slice_in_dim(lax.dynamic_index_in_dim(partials, arc_id, 0, False), start, EPOCH_DEV, 1)
        return local_terms(trans_shard, forcing_shard, partial_shard)
    to_entry, local_sum = lax.map(one_shard, shard_ids)
    to_entry = to_entry.reshape(ARCS, TSHARDS, 6, EPOCH_DEV + 6)
    local_sum = local_sum.reshape(ARCS, TSHARDS, EPOCH_DEV + 6, COEFFS)
    summary_maps = jnp.swapaxes(to_entry[:, :, :, EPOCH_DEV:], 2, 3)
    summary_forcing = local_sum[:, :, EPOCH_DEV:, :]

    def advance(carried, item):
        combined = (jnp.einsum('nab,nbc->nac', item[0], carried[0], precision=exact_precision), jnp.einsum('nab,nbc->nac', item[0], carried[1], precision=exact_precision) + item[1])
        return (combined, carried)
    initial = (jnp.broadcast_to(jnp.eye(6, dtype=jnp.float32), (ARCS, 6, 6)), jnp.zeros((ARCS, 6, COEFFS), jnp.float32))
    final_state, entries = lax.scan(advance, initial, (jnp.swapaxes(summary_maps, 0, 1), jnp.swapaxes(summary_forcing, 0, 1)))
    entry_maps = jnp.swapaxes(entries[0], 0, 1)
    entry_forcing = jnp.swapaxes(entries[1], 0, 1)
    lead_vectors = to_entry[:, :, :, :EPOCH_DEV]
    row_state = jnp.einsum('ntak,ntac->ntkc', lead_vectors, entry_maps, precision=exact_precision)
    row_coeff = local_sum[:, :, :EPOCH_DEV, :] + jnp.einsum('ntak,ntac->ntkc', lead_vectors, entry_forcing, precision=exact_precision)
    obs_rows = observed.reshape(ARCS, TSHARDS, EPOCH_DEV)
    active = jnp.arange(EPOCH_DEV, dtype=jnp.int32)[None, None, :] < counts[:, :, None]
    weighted = jnp.where(active[:, :, :, None], row_state, jnp.float32(0.0))
    information = jnp.einsum('ntkb,ntkc->nbc', weighted, row_state, precision=exact_precision) + jnp.eye(6, dtype=jnp.float32)
    coupling = jnp.einsum('ntkb,ntkc->nbc', weighted, row_coeff, precision=exact_precision)
    coupling_obs = jnp.einsum('ntkb,ntk->nb', weighted, obs_rows, precision=exact_precision)
    solved = solve_small(information, coupling)
    solved_obs = solve_small(information, coupling_obs[:, :, None])[:, :, 0]
    reduced = jnp.where(active[:, :, :, None], row_coeff - jnp.einsum('ntkb,nbc->ntkc', row_state, solved, precision=exact_precision), jnp.float32(0.0)).astype(jnp.bfloat16)
    reduced_obs = jnp.where(active, obs_rows - jnp.einsum('ntkb,nb->ntk', row_state, solved_obs, precision=exact_precision), jnp.float32(0.0)).astype(jnp.bfloat16)
    weighting = 1.0 / (ARCS * EPOCHS)
    flat_rows = reduced.reshape(ARCS * EPOCHS, COEFFS)
    flat_obs = reduced_obs.reshape(ARCS * EPOCHS)
    rhs = jnp.dot(flat_obs.astype(jnp.float32), flat_rows.astype(jnp.float32), preferred_element_type=jnp.float32) * weighting

    def one_block(block_id):
        block_cols = lax.dynamic_slice_in_dim(flat_rows, (block_id * BLOCK).astype(jnp.int32), BLOCK, 1).astype(jnp.float32)
        return jnp.dot(block_cols.T, block_cols, precision=exact_precision) * weighting
    gram = lax.map(one_block, jnp.arange(ARCS, dtype=jnp.int32)).reshape(COEFFS, BLOCK)
    return (gram, rhs)
```

```python
import jax
import jax.numpy as jnp
from jax import lax
from jax.experimental import pallas as pl
from jax.experimental.pallas import tpu as pltpu
from jax.sharding import PartitionSpec as P

EP = 32
BLK = 1152
HALF = 576
SLICE = 72
ROWS = 48
OUT_ROWS = 80
TS = 16
AUG = 128
WIDE = BLK + AUG
f32 = jnp.float32
bf16 = jnp.bfloat16


def rounded(x):
    return x.astype(bf16).astype(f32)


def pack_kernel(cnt_ref, tr_ref, pa_ref, ob_ref, f_hbm, out_ref, fbuf, wt_ref, w_ref, blk_ref, sm_ref, sems):
    j = pl.program_id(0)
    n_blocks = fbuf.shape[0]

    def fetch(b):
        return pltpu.make_async_copy(f_hbm.at[:, :, pl.ds(b * BLK, BLK)], fbuf.at[b], sems.at[b])

    @pl.when(j == 0)
    def _():
        for b in range(n_blocks):
            fetch(b).start()
        lane = lax.broadcasted_iota(jnp.int32, (6, 128), 1)
        sub = lax.broadcasted_iota(jnp.int32, (6, 128), 0)
        sm_ref[...] = jnp.zeros_like(sm_ref)
        sm_ref[0:6, 0:EP] = pa_ref[...]
        heads = sm_ref[0:6, :]
        rows = jnp.where(lane == sub + EP, f32(1.0), f32(0.0))
        for i in range(EP - 1, -1, -1):
            wt_ref[:, i, :] = rows
            new = None
            for c in range(6):
                term = tr_ref[c, :, i : i + 1] * rows[c : c + 1, :]
                new = term if new is None else new + term
            rows = jnp.where(lane == i, heads, new)
        sm_ref[0:6, :] = rows
        sm_ref[6:7, 0:EP] = ob_ref[...]
        lane1 = lax.broadcasted_iota(jnp.int32, (1, 128), 1)
        sm_ref[7:8, :] = jnp.where((lane1 < EP) & (lane1 < cnt_ref[0, 0]), f32(1.0), f32(0.0))
        weights = jnp.transpose(wt_ref[...].reshape(6 * EP, 128))
        w_ref[...] = weights[0:ROWS, :].astype(bf16)
        small = jnp.concatenate([sm_ref[b : b + 1, :] for b in range(8)] + [jnp.zeros((1, 128), f32)], axis=1)
        high = rounded(small)
        middle = rounded(small - high)
        blk_ref[...] = jnp.zeros_like(blk_ref)
        blk_ref[38:39, :] = high
        blk_ref[39:40, :] = middle
        blk_ref[46:47, :] = small - high - middle

    fetch(j).wait()
    local = jnp.dot(w_ref[...], fbuf[j].reshape(6 * EP, BLK), preferred_element_type=f32)
    blk_ref[0:38, :] = local[0:38, :]
    summary = local[32:38, :]
    blk_ref[40:46, :] = summary - rounded(summary)
    packed = blk_ref[...].astype(bf16)
    out_ref[0] = packed
    out_ref[1] = packed


def pack(counts, transition, partials, observed, forcing):
    n_blocks = forcing.shape[2] // BLK
    return pl.pallas_call(
        pack_kernel,
        grid=(n_blocks,),
        out_shape=jax.ShapeDtypeStruct((2 * n_blocks, ROWS, BLK), bf16),
        in_specs=[
            pl.BlockSpec(memory_space=pltpu.SMEM),
            pl.BlockSpec((6, 6, EP), lambda j: (0, 0, 0)),
            pl.BlockSpec((6, EP), lambda j: (0, 0)),
            pl.BlockSpec((1, EP), lambda j: (0, 0)),
            pl.BlockSpec(memory_space=pl.ANY),
        ],
        out_specs=pl.BlockSpec((2, ROWS, BLK), lambda j: (j, 0, 0)),
        scratch_shapes=[
            pltpu.VMEM((n_blocks, 6, EP, BLK), bf16),
            pltpu.VMEM((6, EP, 128), f32),
            pltpu.VMEM((ROWS, 6 * EP), bf16),
            pltpu.VMEM((ROWS, BLK), f32),
            pltpu.VMEM((8, 128), f32),
            pltpu.SemaphoreType.DMA((n_blocks,)),
        ],
        compiler_params=pltpu.CompilerParams(vmem_limit_bytes=32 << 20),
        name="pack_rows",
    )(counts, transition, partials, observed, forcing)


def normal_kernel(place_ref, r_ref, keep_ref, send_ref, te_ref, tt_ref, in_ref, y_ref, n_ref, x_ref, l_ref, g_ref, rr_ref):
    half = place_ref[0]
    core = place_ref[1]
    rows_of = [r_ref[t, 32:48, :].astype(f32) for t in range(TS)]
    for t in range(TS):
        both = rows_of[t][0:8, :] + rows_of[t][8:16, :]
        small = both[6:7, :] + both[7:8, :]
        for b in range(8):
            te_ref[8 * t + b : 8 * t + b + 1, :] = small[:, 128 * b : 128 * b + 128]
    turned = jnp.transpose(te_ref[...])[0:40, :]
    for t in range(TS):
        tt_ref[t] = turned if t == 0 else pltpu.roll(turned, 128 - 8 * t, 1)

    sub = lax.broadcasted_iota(jnp.int32, (8, BLK), 0)
    subw = lax.broadcasted_iota(jnp.int32, (8, WIDE), 0)
    lanew = lax.broadcasted_iota(jnp.int32, (8, WIDE), 1)
    state = jnp.where((lanew == subw + BLK) & (subw < 6), f32(1.0), f32(0.0))
    for t in range(TS):
        in_ref[t] = state
        if t == TS - 1:
            break
        both = rows_of[t][0:8, :] + rows_of[t][8:16, :]
        both = jnp.where(sub < 6, both, f32(0.0))
        new = jnp.concatenate([both, jnp.zeros((8, AUG), f32)], axis=1)
        for b in range(6):
            new = new + tt_ref[t, 32:40, b : b + 1] * state[b : b + 1, :]
        state = new

    lane_aug = lax.broadcasted_iota(jnp.int32, (EP, AUG), 1)

    def rows_step(t, carry):
        coef = tt_ref[t, 0:EP, :]
        active = coef[:, 7:8] > f32(0.5)
        base = jnp.concatenate(
            [r_ref[t, 0:EP, :].astype(f32), jnp.where(lane_aug == 6, coef[:, 6:7], f32(0.0))], axis=1
        )
        for b in range(6):
            base = base + coef[:, b : b + 1] * in_ref[t, b : b + 1, :]
        y_ref[pl.ds(pl.multiple_of(t * EP, EP), EP), :] = jnp.where(active, base, f32(0.0))
        return carry

    lax.fori_loop(0, TS, rows_step, 0)

    aug = y_ref[:, BLK:WIDE]
    lane_all = lax.broadcasted_iota(jnp.int32, aug.shape, 1)
    states = jnp.where(lane_all < 6, aug, f32(0.0))
    high = states.astype(bf16)
    low = (states - high.astype(f32)).astype(bf16)
    low_aug = (aug - rounded(aug)).astype(bf16)
    dims = (((0,), (0,)), ((), ()))
    whole = y_ref[...].astype(bf16)
    right = jnp.concatenate([whole, low_aug], axis=1)
    n_high = lax.dot_general(high, right, dims, preferred_element_type=f32)[0:8]
    n_low = lax.dot_general(low, right, dims, preferred_element_type=f32)[0:8]
    total = n_high + n_low
    augmented = total[:, BLK:WIDE] + total[:, WIDE:]
    eye = jnp.where(
        (lax.broadcasted_iota(jnp.int32, (8, AUG), 1) == lax.broadcasted_iota(jnp.int32, (8, AUG), 0)), f32(1.0), f32(0.0)
    )
    system = jnp.concatenate([total[:, 0:BLK], augmented + eye], axis=1)
    row_id = lax.broadcasted_iota(jnp.int32, (8, WIDE), 0)
    for p in range(6):
        column = system[:, BLK + p : BLK + p + 1]
        pivot = system[p : p + 1, :] / system[p : p + 1, BLK + p : BLK + p + 1]
        system = jnp.where(row_id == p, pivot, system - column * pivot)
    n_ref[...] = system

    def reduce_step(t, carry):
        at = pl.ds(pl.multiple_of(t * EP, EP), EP)
        rows = y_ref[at, :]
        coef = rows[:, BLK:WIDE]
        for b in range(6):
            rows = rows - coef[:, b : b + 1] * n_ref[b : b + 1, :]
        x_ref[at, :] = rows[:, 0:BLK].astype(bf16)
        tail = jnp.where(lane_aug == 6, rows[:, BLK:WIDE], f32(0.0))
        l_ref[at, HALF : HALF + 64] = pltpu.roll(tail, 122, 1)[:, 0:64].astype(bf16)
        return carry

    lax.fori_loop(0, TS, reduce_step, 0)

    @pl.when(half == 0)
    def _():
        l_ref[:, 0:HALF] = x_ref[:, 0:HALF]

    @pl.when(half == 1)
    def _():
        l_ref[:, 0:HALF] = x_ref[:, HALF:BLK]

    scale = f32(1.0 / 4096.0)
    g_ref[...] = lax.dot_general(l_ref[...], x_ref[...], dims, preferred_element_type=f32) * scale

    @pl.when(half == 0)
    def _():
        rr_ref[...] = g_ref[HALF : HALF + 8, 0:HALF]

    @pl.when(half == 1)
    def _():
        rr_ref[...] = g_ref[HALF : HALF + 8, HALF:BLK]

    for s in range(8):
        q, parity = s // 2, s % 2
        side = rr_ref[:, SLICE * s : SLICE * (s + 1)]
        extra = jnp.concatenate([side, jnp.zeros((8, BLK - SLICE), f32)], axis=1)
        block = jnp.concatenate([g_ref[SLICE * s : SLICE * (s + 1), :], extra], axis=0)

        @pl.when(core == parity)
        def _():
            keep_ref[q] = block

        @pl.when(core != parity)
        def _():
            send_ref[q] = block.astype(bf16)


def normals(place, received):
    return pl.pallas_call(
        normal_kernel,
        out_shape=(
            jax.ShapeDtypeStruct((4, OUT_ROWS, BLK), f32),
            jax.ShapeDtypeStruct((4, OUT_ROWS, BLK), bf16),
        ),
        in_specs=[pl.BlockSpec(memory_space=pltpu.SMEM), pl.BlockSpec(memory_space=pltpu.VMEM)],
        out_specs=(pl.BlockSpec(memory_space=pltpu.VMEM), pl.BlockSpec(memory_space=pltpu.VMEM)),
        scratch_shapes=[
            pltpu.VMEM((128, 128), f32),
            pltpu.VMEM((TS, 40, 128), f32),
            pltpu.VMEM((TS, 8, WIDE), f32),
            pltpu.VMEM((TS * EP, WIDE), f32),
            pltpu.VMEM((8, WIDE), f32),
            pltpu.VMEM((TS * EP, BLK), bf16),
            pltpu.VMEM((TS * EP, HALF + 64), bf16),
            pltpu.VMEM((HALF + 64, BLK), f32),
            pltpu.VMEM((8, HALF), f32),
        ],
        compiler_params=pltpu.CompilerParams(vmem_limit_bytes=40 << 20),
        name="normal_rows",
    )(place, received)


def local(transition, forcing, partials, observed, counts):
    packed = pack(counts, transition[0], partials[0], observed, jnp.transpose(forcing[0], (1, 0, 2)))
    received = lax.all_to_all(packed, "tm", split_axis=0, concat_axis=0, tiled=True)
    arc, tm = lax.axis_index("arc"), lax.axis_index("tm")
    place = jnp.stack([tm % 2, arc % 2]).astype(jnp.int32)
    keep, send = normals(place, received)
    arcs, shards = lax.axis_size("arc"), lax.axis_size("tm")
    other_core = [(a * shards + t, (a ^ 1) * shards + t) for a in range(arcs) for t in range(shards)]
    arrived = lax.ppermute(send, ("arc", "tm"), other_core)
    pair_sum = (keep + arrived.astype(f32)).astype(bf16)
    same_core = [[c + 2 * z for z in range(arcs // 2)] for c in range(2)]
    slices = lax.all_to_all(pair_sum, "arc", split_axis=0, concat_axis=0, tiled=True, axis_index_groups=same_core)
    mine = jnp.sum(slices.astype(f32), axis=0).astype(bf16)
    to_owner = [
        (a * shards + t, (t // 2) * shards + 8 * (t % 2) + a) for a in range(arcs) for t in range(shards)
    ]
    final = lax.ppermute(mine, ("arc", "tm"), to_owner).astype(f32)
    return final[0:SLICE, :], final[SLICE, 0:SLICE]


def solution(mesh):
    return jax.shard_map(
        local,
        mesh=mesh,
        in_specs=(
            P("arc", None, None, "tm"),
            P("arc", "tm", None, None),
            P("arc", None, "tm"),
            P("arc", "tm"),
            P("arc", "tm"),
        ),
        out_specs=(P(("arc", "tm"), None), P(("arc", "tm"))),
        check_vma=False,
    )
```

```python
import jax
import jax.numpy as jnp
from jax import lax
from jax.experimental import pallas as pl
from jax.experimental.pallas import tpu as pltpu
from jax.sharding import PartitionSpec as P

EP = 32
BLK = 1152
HALF = 576
SLICE = 72
ROWS = 40
OUT_ROWS = 80
TS = 16
AUG = 128
WIDE = BLK + AUG
f32 = jnp.float32
bf16 = jnp.bfloat16


def rounded(x):
    return x.astype(bf16).astype(f32)


def pack_kernel(
    cnt_ref, tr_hbm, pa_hbm, ob_hbm, f_hbm, out_ref,
    tr_ref, pa_ref, ob_ref, fbuf, wt_ref, w_ref, blk_ref, sm_ref, sems, small_sems,
):
    j = pl.program_id(0)
    n_blocks = fbuf.shape[0]

    def fetch(b):
        return pltpu.make_async_copy(f_hbm.at[:, :, pl.ds(b * BLK, BLK)], fbuf.at[b], sems.at[b])

    @pl.when(j == 0)
    def _():
        smalls = [
            pltpu.make_async_copy(src, dst, small_sems.at[n])
            for n, (src, dst) in enumerate(((tr_hbm, tr_ref), (pa_hbm, pa_ref), (ob_hbm, ob_ref)))
        ]
        for copy in smalls:
            copy.start()
        for b in range(n_blocks):
            fetch(b).start()
        lane = lax.broadcasted_iota(jnp.int32, (6, 128), 1)
        sub = lax.broadcasted_iota(jnp.int32, (6, 128), 0)
        sm_ref[...] = jnp.zeros_like(sm_ref)
        blk_ref[...] = jnp.zeros_like(blk_ref)
        for copy in smalls:
            copy.wait()
        for b in range(6):
            sm_ref[b : b + 1, 0:EP] = pa_ref[b]
        heads = sm_ref[0:6, :]
        rows = jnp.where(lane == sub + EP, f32(1.0), f32(0.0))
        steps = [tr_ref[c, :, 0, :] for c in range(6)]
        for i in range(EP - 1, -1, -1):
            wt_ref[:, i, :] = rows
            terms = [steps[c][:, i : i + 1] * rows[c : c + 1, :] for c in range(6)]
            new = ((terms[0] + terms[1]) + (terms[2] + terms[3])) + (terms[4] + terms[5])
            rows = jnp.where(lane == i, heads, new)
        sm_ref[0:6, :] = rows
        sm_ref[6:7, 0:EP] = ob_ref[...]
        lane1 = lax.broadcasted_iota(jnp.int32, (1, 128), 1)
        sm_ref[7:8, :] = jnp.where((lane1 < EP) & (lane1 < cnt_ref[0, 0]), f32(1.0), f32(0.0))
        weights = jnp.transpose(wt_ref[...].reshape(6 * EP, 128))
        w_ref[...] = weights[0:ROWS, :].astype(bf16)
        small = jnp.concatenate([sm_ref[b : b + 1, :] for b in range(8)] + [jnp.zeros((1, 128), f32)], axis=1)
        high = rounded(small)
        blk_ref[38:39, :] = high
        blk_ref[39:40, :] = small - high

    fetch(j).wait()
    local = jnp.dot(w_ref[...], fbuf[j].reshape(6 * EP, BLK), preferred_element_type=f32)
    blk_ref[0:38, :] = local[0:38, :]
    packed = blk_ref[...].astype(bf16)
    out_ref[0, 0, 0] = packed
    out_ref[0, 1, 0] = packed


def pack(counts, transition, partials, observed, forcing):
    n_blocks = forcing.shape[2] // BLK
    hbm = pl.BlockSpec(memory_space=pl.ANY)
    return pl.pallas_call(
        pack_kernel,
        grid=(n_blocks,),
        out_shape=jax.ShapeDtypeStruct((n_blocks // 2, 2, 2, ROWS, BLK), bf16),
        in_specs=[pl.BlockSpec(memory_space=pltpu.SMEM), hbm, hbm, hbm, hbm],
        out_specs=pl.BlockSpec((1, 2, 1, ROWS, BLK), lambda j: (j // 2, 0, j % 2, 0, 0)),
        scratch_shapes=[
            pltpu.VMEM((6, 6, 1, EP), f32),
            pltpu.VMEM((6, 1, EP), f32),
            pltpu.VMEM((1, EP), f32),
            pltpu.VMEM((n_blocks, 6, EP, BLK), bf16),
            pltpu.VMEM((6, EP, 128), f32),
            pltpu.VMEM((ROWS, 6 * EP), bf16),
            pltpu.VMEM((ROWS, BLK), f32),
            pltpu.VMEM((8, 128), f32),
            pltpu.SemaphoreType.DMA((n_blocks,)),
            pltpu.SemaphoreType.DMA((3,)),
        ],
        compiler_params=pltpu.CompilerParams(vmem_limit_bytes=58 << 20),
        name="pack_rows",
    )(counts, transition, partials, observed, forcing).reshape(2 * n_blocks, ROWS, BLK)


def normal_kernel(place_ref, r_ref, keep_ref, send_ref, te_ref, tt_ref, in_ref, y_ref, n_ref, x_ref, l_ref, g_ref, rr_ref):
    half = place_ref[0]
    core = place_ref[1]
    turn = place_ref[2]
    rows_of = [r_ref[t, 32:40, :].astype(f32) for t in range(TS)]
    for t in range(TS):
        small = rows_of[t][6:7, :] + rows_of[t][7:8, :]
        for b in range(8):
            te_ref[8 * t + b : 8 * t + b + 1, :] = small[:, 128 * b : 128 * b + 128]
    turned = jnp.transpose(te_ref[...])[0:40, :]
    for t in range(TS):
        tt_ref[t] = turned if t == 0 else pltpu.roll(turned, 128 - 8 * t, 1)

    sub = lax.broadcasted_iota(jnp.int32, (8, BLK), 0)
    subw = lax.broadcasted_iota(jnp.int32, (8, WIDE), 0)
    lanew = lax.broadcasted_iota(jnp.int32, (8, WIDE), 1)
    state = jnp.where((lanew == subw + BLK) & (subw < 6), f32(1.0), f32(0.0))
    for t in range(TS):
        in_ref[t] = state
        if t == TS - 1:
            break
        both = jnp.where(sub < 6, rows_of[t], f32(0.0))
        new = jnp.concatenate([both, jnp.zeros((8, AUG), f32)], axis=1)
        for b in range(6):
            new = new + tt_ref[t, 32:40, b : b + 1] * state[b : b + 1, :]
        state = new

    lane_aug = lax.broadcasted_iota(jnp.int32, (EP, AUG), 1)

    def rows_step(t, carry):
        coef = tt_ref[t, 0:EP, :]
        active = coef[:, 7:8] > f32(0.5)
        base = jnp.concatenate(
            [r_ref[t, 0:EP, :].astype(f32), jnp.where(lane_aug == 6, coef[:, 6:7], f32(0.0))], axis=1
        )
        for b in range(6):
            base = base + coef[:, b : b + 1] * in_ref[t, b : b + 1, :]
        y_ref[pl.ds(pl.multiple_of(t * EP, EP), EP), :] = jnp.where(active, base, f32(0.0))
        return carry

    lax.fori_loop(0, TS, rows_step, 0)

    aug = y_ref[:, BLK:WIDE]
    lane_all = lax.broadcasted_iota(jnp.int32, aug.shape, 1)
    states = jnp.where(lane_all < 6, aug, f32(0.0))
    high = states.astype(bf16)
    low = (states - high.astype(f32)).astype(bf16)
    low_aug = (aug - rounded(aug)).astype(bf16)
    dims = (((0,), (0,)), ((), ()))
    whole = y_ref[...].astype(bf16)
    right = jnp.concatenate([whole, low_aug], axis=1)
    n_high = lax.dot_general(high, right, dims, preferred_element_type=f32)[0:8]
    n_low = lax.dot_general(low, right, dims, preferred_element_type=f32)[0:8]
    total = n_high + n_low
    augmented = total[:, BLK:WIDE] + total[:, WIDE:]
    eye = jnp.where(
        (lax.broadcasted_iota(jnp.int32, (8, AUG), 1) == lax.broadcasted_iota(jnp.int32, (8, AUG), 0)), f32(1.0), f32(0.0)
    )
    system = jnp.concatenate([total[:, 0:BLK], augmented + eye], axis=1)
    row_id = lax.broadcasted_iota(jnp.int32, (8, WIDE), 0)
    for p in range(6):
        column = system[:, BLK + p : BLK + p + 1]
        pivot = system[p : p + 1, :] / system[p : p + 1, BLK + p : BLK + p + 1]
        system = jnp.where(row_id == p, pivot, system - column * pivot)
    n_ref[...] = system

    def reduce_step(t, carry):
        at = pl.ds(pl.multiple_of(t * EP, EP), EP)
        rows = y_ref[at, :]
        coef = rows[:, BLK:WIDE]
        for b in range(6):
            rows = rows - coef[:, b : b + 1] * n_ref[b : b + 1, :]
        x_ref[at, :] = rows[:, 0:BLK].astype(bf16)
        tail = jnp.where(lane_aug == 6, rows[:, BLK:WIDE], f32(0.0))
        l_ref[at, HALF : HALF + 64] = pltpu.roll(tail, 122, 1)[:, 0:64].astype(bf16)
        return carry

    lax.fori_loop(0, TS, reduce_step, 0)

    for side in range(2):

        @pl.when(half == side)
        def _():
            for q in range(4):
                l_ref[:, 2 * SLICE * q : 2 * SLICE * (q + 1)] = x_ref[
                    :, 4 * SLICE * q + 2 * SLICE * side : 4 * SLICE * q + 2 * SLICE * (side + 1)
                ]

    scale = f32(1.0 / 4096.0)
    g_ref[...] = lax.dot_general(l_ref[...], x_ref[...], dims, preferred_element_type=f32) * scale

    for side in range(2):

        @pl.when(half == side)
        def _():
            for q in range(4):
                first = 4 * SLICE * q + 2 * SLICE * side
                rr_ref[:, 2 * SLICE * q : 2 * SLICE * (q + 1)] = g_ref[HALF : HALF + 8, first : first + 2 * SLICE]

    for s in range(8):
        slot, parity = lax.rem(s // 2 + 4 - turn, 4), s % 2
        beside = rr_ref[:, SLICE * s : SLICE * (s + 1)]
        extra = jnp.concatenate([beside, jnp.zeros((8, BLK - SLICE), f32)], axis=1)
        block = jnp.concatenate([g_ref[SLICE * s : SLICE * (s + 1), :], extra], axis=0)

        @pl.when(core == parity)
        def _():
            keep_ref[slot] = block

        @pl.when(core != parity)
        def _():
            send_ref[slot] = block.astype(bf16)


def normals(place, received):
    return pl.pallas_call(
        normal_kernel,
        out_shape=(
            jax.ShapeDtypeStruct((4, OUT_ROWS, BLK), f32),
            jax.ShapeDtypeStruct((4, OUT_ROWS, BLK), bf16),
        ),
        in_specs=[pl.BlockSpec(memory_space=pltpu.SMEM), pl.BlockSpec(memory_space=pltpu.VMEM)],
        out_specs=(pl.BlockSpec(memory_space=pltpu.VMEM), pl.BlockSpec(memory_space=pltpu.VMEM)),
        scratch_shapes=[
            pltpu.VMEM((128, 128), f32),
            pltpu.VMEM((TS, 40, 128), f32),
            pltpu.VMEM((TS, 8, WIDE), f32),
            pltpu.VMEM((TS * EP, WIDE), f32),
            pltpu.VMEM((8, WIDE), f32),
            pltpu.VMEM((TS * EP, BLK), bf16),
            pltpu.VMEM((TS * EP, HALF + 64), bf16),
            pltpu.VMEM((HALF + 64, BLK), f32),
            pltpu.VMEM((8, HALF), f32),
        ],
        compiler_params=pltpu.CompilerParams(vmem_limit_bytes=40 << 20),
        name="normal_rows",
    )(place, received)


def local(transition, forcing, partials, observed, counts):
    packed = pack(
        counts,
        jnp.transpose(transition, (1, 2, 0, 3)),
        jnp.transpose(partials, (1, 0, 2)),
        observed,
        jnp.transpose(forcing[0], (1, 0, 2)),
    )
    received = lax.all_to_all(packed, "tm", split_axis=0, concat_axis=0, tiled=True)
    arc, tm = lax.axis_index("arc"), lax.axis_index("tm")
    place = jnp.stack([tm % 4 // 2, arc % 2, tm // 4]).astype(jnp.int32)
    keep, send = normals(place, received)
    arcs, shards = lax.axis_size("arc"), lax.axis_size("tm")
    other_core = [(a * shards + t, (a ^ 1) * shards + t) for a in range(arcs) for t in range(shards)]
    arrived = lax.ppermute(send, ("arc", "tm"), other_core)
    pair_sum = (keep + arrived.astype(f32)).astype(bf16)
    same_core = [[c + 2 * z for z in range(arcs // 2)] for c in range(2)]
    slices = lax.all_to_all(pair_sum, "arc", split_axis=0, concat_axis=0, tiled=True, axis_index_groups=same_core)
    mine = jnp.sum(slices.astype(f32), axis=0).astype(bf16)
    to_owner = []
    for a in range(arcs):
        for t in range(shards):
            z, c, y, h, odd = a // 2, a % 2, t // 4, t % 4 // 2, t % 2
            to_owner.append((a * shards + t, (2 * y + odd) * shards + (y + z) % 4 * 4 + 2 * h + c))
    final = lax.ppermute(mine, ("arc", "tm"), to_owner).astype(f32)
    return final[0:SLICE, :], final[SLICE, 0:SLICE]


def solution(mesh):
    return jax.shard_map(
        local,
        mesh=mesh,
        in_specs=(
            P("arc", None, None, "tm"),
            P("arc", "tm", None, None),
            P("arc", None, "tm"),
            P("arc", "tm"),
            P("arc", "tm"),
        ),
        out_specs=(P(("arc", "tm"), None), P(("arc", "tm"))),
        check_vma=False,
    )
```

```python
import jax
import jax.numpy as jnp
from jax import lax
from jax.experimental import pallas as pl
from jax.experimental.pallas import tpu as pltpu
from jax.sharding import PartitionSpec as P

EP = 32
BLK = 1152
HALF = 576
SLICE = 72
ROWS = 40
OUT_ROWS = 80
TS = 16
AUG = 128
WIDE = BLK + AUG
f32 = jnp.float32
bf16 = jnp.bfloat16


def rounded(x):
    return x.astype(bf16).astype(f32)


def pack_kernel(
    cnt_ref, tr_hbm, pa_hbm, ob_hbm, f_hbm, out_ref, tr_ref, pa_ref, ob_ref, fbuf, wt_ref, sm_ref, sems, small_sems
):
    n_blocks = fbuf.shape[0]
    smalls = [
        pltpu.make_async_copy(src, dst, small_sems.at[n])
        for n, (src, dst) in enumerate(((tr_hbm, tr_ref), (pa_hbm, pa_ref), (ob_hbm, ob_ref)))
    ]
    for copy in smalls:
        copy.start()
    fetches = [
        pltpu.make_async_copy(f_hbm.at[:, :, pl.ds(b * BLK, BLK)], fbuf.at[b], sems.at[b]) for b in range(n_blocks)
    ]
    for copy in fetches:
        copy.start()
    lane = lax.broadcasted_iota(jnp.int32, (6, 128), 1)
    sub = lax.broadcasted_iota(jnp.int32, (6, 128), 0)
    sm_ref[...] = jnp.zeros_like(sm_ref)
    for copy in smalls:
        copy.wait()
    for b in range(6):
        sm_ref[b : b + 1, 0:EP] = pa_ref[b]
    heads = sm_ref[0:6, :]
    rows = jnp.where(lane == sub + EP, f32(1.0), f32(0.0))
    steps = [tr_ref[c, :, 0, :] for c in range(6)]
    for i in range(EP - 1, -1, -1):
        wt_ref[:, i, :] = rows
        terms = [steps[c][:, i : i + 1] * rows[c : c + 1, :] for c in range(6)]
        new = ((terms[0] + terms[1]) + (terms[2] + terms[3])) + (terms[4] + terms[5])
        rows = jnp.where(lane == i, heads, new)
    sm_ref[0:6, :] = rows
    sm_ref[6:7, 0:EP] = ob_ref[...]
    lane1 = lax.broadcasted_iota(jnp.int32, (1, 128), 1)
    sm_ref[7:8, :] = jnp.where((lane1 < EP) & (lane1 < cnt_ref[0, 0]), f32(1.0), f32(0.0))
    weights = jnp.transpose(wt_ref[...].reshape(6 * EP, 128))[0:ROWS, :].astype(bf16)
    small = jnp.concatenate([sm_ref[b : b + 1, :] for b in range(8)] + [jnp.zeros((1, 128), f32)], axis=1)
    high = rounded(small)
    row = lax.broadcasted_iota(jnp.int32, (8, BLK), 0)
    tail = jnp.where(row == 6, high, jnp.where(row == 7, small - high, f32(0.0)))
    for b in range(n_blocks):
        fetches[b].wait()
        local = jnp.dot(weights, fbuf[b].reshape(6 * EP, BLK), preferred_element_type=f32)
        packed = jnp.concatenate([local[0:EP, :], local[EP:ROWS, :] + tail], axis=0).astype(bf16)
        for h in range(2):
            out_ref[b // 2 * 4 + 2 * h + b % 2] = packed


def pack(counts, transition, partials, observed, forcing):
    n_blocks = forcing.shape[2] // BLK
    hbm = pl.BlockSpec(memory_space=pltpu.MemorySpace.HBM)
    return pl.pallas_call(
        pack_kernel,
        out_shape=jax.ShapeDtypeStruct((2 * n_blocks, ROWS, BLK), bf16),
        in_specs=[pl.BlockSpec(memory_space=pltpu.SMEM), hbm, hbm, hbm, hbm],
        out_specs=pl.BlockSpec(memory_space=pltpu.VMEM),
        scratch_shapes=[
            pltpu.VMEM((6, 6, 1, EP), f32),
            pltpu.VMEM((6, 1, EP), f32),
            pltpu.VMEM((1, EP), f32),
            pltpu.VMEM((n_blocks, 6, EP, BLK), bf16),
            pltpu.VMEM((6, EP, 128), f32),
            pltpu.VMEM((8, 128), f32),
            pltpu.SemaphoreType.DMA((n_blocks,)),
            pltpu.SemaphoreType.DMA((3,)),
        ],
        compiler_params=pltpu.CompilerParams(vmem_limit_bytes=32 << 20),
        name="pack_rows",
    )(counts, *[pltpu.with_memory_space_constraint(x, pltpu.MemorySpace.HBM) for x in (transition, partials, observed, forcing)])


def normal_kernel(r_ref, keep_ref, send_ref, te_ref, tt_ref, in_ref, y_ref, n_ref, x_ref, l_ref, g_ref, rr_ref):
    shard = lax.axis_index("tm")
    half = lax.div(lax.rem(shard, 4), 2)
    turn = lax.div(shard, 4)
    core = lax.rem(lax.axis_index("arc"), 2)
    rows_of = [r_ref[t, 32:40, :].astype(f32) for t in range(TS)]
    for t in range(TS):
        small = rows_of[t][6:7, :] + rows_of[t][7:8, :]
        for b in range(8):
            te_ref[8 * t + b : 8 * t + b + 1, :] = small[:, 128 * b : 128 * b + 128]
    turned = jnp.transpose(te_ref[...])[0:40, :]
    for t in range(TS):
        tt_ref[t] = turned if t == 0 else pltpu.roll(turned, 128 - 8 * t, 1)

    sub = lax.broadcasted_iota(jnp.int32, (8, BLK), 0)
    subw = lax.broadcasted_iota(jnp.int32, (8, WIDE), 0)
    lanew = lax.broadcasted_iota(jnp.int32, (8, WIDE), 1)
    state = jnp.where((lanew == subw + BLK) & (subw < 6), f32(1.0), f32(0.0))
    for t in range(TS):
        in_ref[t] = state
        if t == TS - 1:
            break
        both = jnp.where(sub < 6, rows_of[t], f32(0.0))
        new = jnp.concatenate([both, jnp.zeros((8, AUG), f32)], axis=1)
        for b in range(6):
            new = new + tt_ref[t, 32:40, b : b + 1] * state[b : b + 1, :]
        state = new

    lane_aug = lax.broadcasted_iota(jnp.int32, (EP, AUG), 1)

    def rows_step(t, carry):
        coef = tt_ref[t, 0:EP, :]
        active = coef[:, 7:8] > f32(0.5)
        base = jnp.concatenate(
            [r_ref[t, 0:EP, :].astype(f32), jnp.where(lane_aug == 6, coef[:, 6:7], f32(0.0))], axis=1
        )
        for b in range(6):
            base = base + coef[:, b : b + 1] * in_ref[t, b : b + 1, :]
        y_ref[pl.ds(pl.multiple_of(t * EP, EP), EP), :] = jnp.where(active, base, f32(0.0))
        return carry

    lax.fori_loop(0, TS, rows_step, 0)

    aug = y_ref[:, BLK:WIDE]
    lane_all = lax.broadcasted_iota(jnp.int32, aug.shape, 1)
    states = jnp.where(lane_all < 6, aug, f32(0.0))
    high = states.astype(bf16)
    low = (states - high.astype(f32)).astype(bf16)
    low_aug = (aug - rounded(aug)).astype(bf16)
    dims = (((0,), (0,)), ((), ()))
    whole = y_ref[...].astype(bf16)
    right = jnp.concatenate([whole, low_aug], axis=1)
    n_high = lax.dot_general(high, right, dims, preferred_element_type=f32)[0:8]
    n_low = lax.dot_general(low, right, dims, preferred_element_type=f32)[0:8]
    total = n_high + n_low
    augmented = total[:, BLK:WIDE] + total[:, WIDE:]
    eye = jnp.where(
        (lax.broadcasted_iota(jnp.int32, (8, AUG), 1) == lax.broadcasted_iota(jnp.int32, (8, AUG), 0)), f32(1.0), f32(0.0)
    )
    system = jnp.concatenate([total[:, 0:BLK], augmented + eye], axis=1)
    row_id = lax.broadcasted_iota(jnp.int32, (8, WIDE), 0)
    for p in range(6):
        column = system[:, BLK + p : BLK + p + 1]
        pivot = system[p : p + 1, :] / system[p : p + 1, BLK + p : BLK + p + 1]
        system = jnp.where(row_id == p, pivot, system - column * pivot)
    n_ref[...] = system

    def reduce_step(t, carry):
        at = pl.ds(pl.multiple_of(t * EP, EP), EP)
        rows = y_ref[at, :]
        coef = rows[:, BLK:WIDE]
        for b in range(6):
            rows = rows - coef[:, b : b + 1] * n_ref[b : b + 1, :]
        x_ref[at, :] = rows[:, 0:BLK].astype(bf16)
        tail = jnp.where(lane_aug == 6, rows[:, BLK:WIDE], f32(0.0))
        l_ref[at, HALF : HALF + 64] = pltpu.roll(tail, 122, 1)[:, 0:64].astype(bf16)
        return carry

    lax.fori_loop(0, TS, reduce_step, 0)

    for side in range(2):

        @pl.when(half == side)
        def _():
            for q in range(4):
                l_ref[:, 2 * SLICE * q : 2 * SLICE * (q + 1)] = x_ref[
                    :, 4 * SLICE * q + 2 * SLICE * side : 4 * SLICE * q + 2 * SLICE * (side + 1)
                ]

    scale = f32(1.0 / 4096.0)
    g_ref[...] = lax.dot_general(l_ref[...], x_ref[...], dims, preferred_element_type=f32) * scale

    for side in range(2):

        @pl.when(half == side)
        def _():
            for q in range(4):
                first = 4 * SLICE * q + 2 * SLICE * side
                rr_ref[:, 2 * SLICE * q : 2 * SLICE * (q + 1)] = g_ref[HALF : HALF + 8, first : first + 2 * SLICE]

    for s in range(8):
        slot, parity = lax.rem(s // 2 + 4 - turn, 4), s % 2
        beside = rr_ref[:, SLICE * s : SLICE * (s + 1)]
        extra = jnp.concatenate([beside, jnp.zeros((8, BLK - SLICE), f32)], axis=1)
        block = jnp.concatenate([g_ref[SLICE * s : SLICE * (s + 1), :], extra], axis=0)

        @pl.when(core == parity)
        def _():
            keep_ref[slot] = block

        @pl.when(core != parity)
        def _():
            send_ref[slot] = block.astype(bf16)


def normals(received):
    return pl.pallas_call(
        normal_kernel,
        out_shape=(
            jax.ShapeDtypeStruct((4, OUT_ROWS, BLK), f32),
            jax.ShapeDtypeStruct((4, OUT_ROWS, BLK), bf16),
        ),
        in_specs=[pl.BlockSpec(memory_space=pltpu.VMEM)],
        out_specs=(pl.BlockSpec(memory_space=pltpu.VMEM), pl.BlockSpec(memory_space=pltpu.VMEM)),
        scratch_shapes=[
            pltpu.VMEM((128, 128), f32),
            pltpu.VMEM((TS, 40, 128), f32),
            pltpu.VMEM((TS, 8, WIDE), f32),
            pltpu.VMEM((TS * EP, WIDE), f32),
            pltpu.VMEM((8, WIDE), f32),
            pltpu.VMEM((TS * EP, BLK), bf16),
            pltpu.VMEM((TS * EP, HALF + 64), bf16),
            pltpu.VMEM((HALF + 64, BLK), f32),
            pltpu.VMEM((8, HALF), f32),
        ],
        compiler_params=pltpu.CompilerParams(vmem_limit_bytes=40 << 20),
        name="normal_rows",
    )(received)


def local(transition, forcing, partials, observed, counts):
    packed = pack(
        counts,
        jnp.transpose(transition, (1, 2, 0, 3)),
        jnp.transpose(partials, (1, 0, 2)),
        observed,
        jnp.transpose(forcing[0], (1, 0, 2)),
    )
    received = lax.all_to_all(packed, "tm", split_axis=0, concat_axis=0, tiled=True)
    keep, send = normals(received)
    arcs, shards = lax.axis_size("arc"), lax.axis_size("tm")
    other_core = [(a * shards + t, (a ^ 1) * shards + t) for a in range(arcs) for t in range(shards)]
    arrived = lax.ppermute(send, ("arc", "tm"), other_core)
    pair_sum = (keep + arrived.astype(f32)).astype(bf16)
    same_core = [[c + 2 * z for z in range(arcs // 2)] for c in range(2)]
    slices = lax.all_to_all(pair_sum, "arc", split_axis=0, concat_axis=0, tiled=True, axis_index_groups=same_core)
    mine = jnp.sum(slices.astype(f32), axis=0).astype(bf16)
    to_owner = []
    for a in range(arcs):
        for t in range(shards):
            z, c, y, h, odd = a // 2, a % 2, t // 4, t % 4 // 2, t % 2
            to_owner.append((a * shards + t, (2 * y + odd) * shards + (y + z) % 4 * 4 + 2 * h + c))
    final = lax.ppermute(mine, ("arc", "tm"), to_owner).astype(f32)
    return final[0:SLICE, :], final[SLICE, 0:SLICE]


def solution(mesh):
    return jax.shard_map(
        local,
        mesh=mesh,
        in_specs=(
            P("arc", None, None, "tm"),
            P("arc", "tm", None, None),
            P("arc", None, "tm"),
            P("arc", "tm"),
            P("arc", "tm"),
        ),
        out_specs=(P(("arc", "tm"), None), P(("arc", "tm"))),
        check_vma=False,
    )
```

```python
import jax
import jax.numpy as jnp
from jax import lax
from jax.experimental import pallas as pl
from jax.experimental.pallas import tpu as pltpu
from jax.sharding import PartitionSpec as P

EP = 32
BLK = 1152
HALF = 576
SLICE = 72
ROWS = 40
OUT_ROWS = 80
TS = 16
AUG = 128
WIDE = BLK + AUG
f32 = jnp.float32
bf16 = jnp.bfloat16


def rounded(x):
    return x.astype(bf16).astype(f32)


def pack_kernel(
    cnt_ref, tr_hbm, pa_hbm, ob_hbm, f_hbm, out_ref, tr_ref, pa_ref, ob_ref, fbuf, wt_ref, sm_ref, sems, small_sems
):
    n_blocks = fbuf.shape[0]
    smalls = [
        pltpu.make_async_copy(src, dst, small_sems.at[n])
        for n, (src, dst) in enumerate(((tr_hbm, tr_ref), (pa_hbm, pa_ref), (ob_hbm, ob_ref)))
    ]
    for copy in smalls:
        copy.start()
    fetches = [
        pltpu.make_async_copy(f_hbm.at[:, :, pl.ds(b * BLK, BLK)], fbuf.at[b], sems.at[b]) for b in range(n_blocks)
    ]
    for copy in fetches:
        copy.start()
    lane = lax.broadcasted_iota(jnp.int32, (6, 128), 1)
    sub = lax.broadcasted_iota(jnp.int32, (6, 128), 0)
    sm_ref[...] = jnp.zeros_like(sm_ref)
    for copy in smalls:
        copy.wait()
    for b in range(6):
        sm_ref[b : b + 1, 0:EP] = pa_ref[b]
    heads = sm_ref[0:6, :]
    rows = jnp.where(lane == sub + EP, f32(1.0), f32(0.0))
    steps = [tr_ref[c, :, 0, :] for c in range(6)]
    for i in range(EP - 1, -1, -1):
        wt_ref[:, i, :] = rows
        terms = [steps[c][:, i : i + 1] * rows[c : c + 1, :] for c in range(6)]
        new = ((terms[0] + terms[1]) + (terms[2] + terms[3])) + (terms[4] + terms[5])
        rows = jnp.where(lane == i, heads, new)
    sm_ref[0:6, :] = rows
    sm_ref[6:7, 0:EP] = ob_ref[...]
    lane1 = lax.broadcasted_iota(jnp.int32, (1, 128), 1)
    sm_ref[7:8, :] = jnp.where((lane1 < EP) & (lane1 < cnt_ref[0, 0]), f32(1.0), f32(0.0))
    weights = jnp.transpose(wt_ref[...].reshape(6 * EP, 128))[0:ROWS, :].astype(bf16)
    small = jnp.concatenate([sm_ref[b : b + 1, :] for b in range(8)] + [jnp.zeros((1, 128), f32)], axis=1)
    high = rounded(small)
    row = lax.broadcasted_iota(jnp.int32, (8, BLK), 0)
    tail = jnp.where(row == 6, high, jnp.where(row == 7, small - high, f32(0.0)))
    for b in range(n_blocks):
        fetches[b].wait()
        local = jnp.dot(weights, fbuf[b].reshape(6 * EP, BLK), preferred_element_type=f32)
        packed = jnp.concatenate([local[0:EP, :], local[EP:ROWS, :] + tail], axis=0).astype(bf16)
        for h in range(2):
            out_ref[b // 2 * 4 + 2 * h + b % 2] = packed


def pack(counts, transition, partials, observed, forcing):
    n_blocks = forcing.shape[2] // BLK
    hbm = pl.BlockSpec(memory_space=pltpu.MemorySpace.HBM)
    return pl.pallas_call(
        pack_kernel,
        out_shape=jax.ShapeDtypeStruct((2 * n_blocks, ROWS, BLK), bf16),
        in_specs=[pl.BlockSpec(memory_space=pltpu.SMEM), hbm, hbm, hbm, hbm],
        out_specs=pl.BlockSpec(memory_space=pltpu.VMEM),
        scratch_shapes=[
            pltpu.VMEM((6, 6, 1, EP), f32),
            pltpu.VMEM((6, 1, EP), f32),
            pltpu.VMEM((1, EP), f32),
            pltpu.VMEM((n_blocks, 6, EP, BLK), bf16),
            pltpu.VMEM((6, EP, 128), f32),
            pltpu.VMEM((8, 128), f32),
            pltpu.SemaphoreType.DMA((n_blocks,)),
            pltpu.SemaphoreType.DMA((3,)),
        ],
        compiler_params=pltpu.CompilerParams(vmem_limit_bytes=32 << 20),
        name="pack_rows",
    )(counts, *[pltpu.with_memory_space_constraint(x, pltpu.MemorySpace.HBM) for x in (transition, partials, observed, forcing)])


def split(x):
    high = x.astype(bf16)
    return high, (x - high.astype(f32)).astype(bf16)


def normal_kernel(r_ref, keep_ref, send_ref, te_ref, in_ref, lead_ref, y_ref, x_ref, l_ref, g_ref, rr_ref):
    shard = lax.axis_index("tm")
    half = lax.div(lax.rem(shard, 4), 2)
    turn = lax.div(shard, 4)
    core = lax.rem(lax.axis_index("arc"), 2)
    dims = (((0,), (0,)), ((), ()))
    tails = [r_ref[t, 32:40, :].astype(f32) for t in range(TS)]
    for t in range(TS):
        small = tails[t][6:7, :] + tails[t][7:8, :]
        for b in range(8):
            te_ref[8 * t + b : 8 * t + b + 1, :] = small[:, 128 * b : 128 * b + 128]
    turned = jnp.transpose(te_ref[...])

    sub = lax.broadcasted_iota(jnp.int32, (8, BLK), 0)
    sub_aug = lax.broadcasted_iota(jnp.int32, (8, AUG), 0)
    lane_aug = lax.broadcasted_iota(jnp.int32, (8, AUG), 1)
    unit = jnp.where((sub_aug == 6) & (lane_aug == 6), f32(1.0), f32(0.0))
    eye = jnp.where((lane_aug == sub_aug) & (sub_aug < 6), f32(1.0), f32(0.0))
    state = jnp.concatenate([jnp.zeros((8, BLK), f32), eye + unit], axis=1)
    for t in range(TS):
        in_ref[8 * t : 8 * t + 8, :] = state
        if t == TS - 1:
            break
        new = jnp.concatenate([jnp.where(sub < 6, tails[t], f32(0.0)), unit], axis=1)
        terms = [turned[32:40, 8 * t + b : 8 * t + b + 1] * state[b : b + 1, :] for b in range(6)]
        state = new + (((terms[0] + terms[1]) + (terms[2] + terms[3])) + (terms[4] + terms[5]))

    lane = lax.broadcasted_iota(jnp.int32, (EP, AUG), 1)
    for t in range(TS):
        active = turned[0:EP, 8 * t + 7 : 8 * t + 8] > f32(0.5)
        mine = (lane >= 8 * t) & (lane < 8 * t + 7) & active
        high, low = split(jnp.where(mine, turned[0:EP, :], f32(0.0)))
        lead_ref[EP * t : EP * t + EP, 0:AUG] = high
        lead_ref[EP * t : EP * t + EP, AUG : 2 * AUG] = low
        lead_ref[EP * t : EP * t + EP, 2 * AUG : 3 * AUG] = high

    maps = in_ref[:, BLK:WIDE]
    maps_high, maps_low = split(maps)
    states = jnp.dot(
        lead_ref[...], jnp.concatenate([maps_high, maps_high, maps_low], axis=0), preferred_element_type=f32
    )
    states_high, states_low = split(states)
    left = (states_high.astype(f32) + pltpu.roll(states_low.astype(f32), 8, 1)).astype(bf16)
    rows = jnp.concatenate([r_ref[t, 0:EP, :] for t in range(TS)], axis=0)
    from_local = lax.dot_general(left, rows, dims, preferred_element_type=f32)
    right = jnp.concatenate([states_high, states_low, lead_ref[:, 0 : 2 * AUG]], axis=1)
    from_small = lax.dot_general(left, right, dims, preferred_element_type=f32)
    from_small = from_small[0:8, :] + from_small[8:16, :]
    augmented = from_small[:, 0:AUG] + from_small[:, AUG : 2 * AUG]
    through = from_small[:, 2 * AUG : 3 * AUG] + from_small[:, 3 * AUG : 4 * AUG]
    through_high, through_low = split(through)
    sums_high, sums_low = split(in_ref[:, 0:BLK])
    from_sums = jnp.dot(
        jnp.concatenate([through_high, through_low, through_high], axis=1),
        jnp.concatenate([sums_high, sums_high, sums_low], axis=0),
        preferred_element_type=f32,
    )
    system = jnp.concatenate([from_local[0:8, :] + from_local[8:16, :] + from_sums, augmented + eye], axis=1)
    row_id = lax.broadcasted_iota(jnp.int32, (8, WIDE), 0)
    for p in range(6):
        column = system[:, BLK + p : BLK + p + 1]
        pivot = system[p : p + 1, :] * (f32(1.0) / system[p : p + 1, BLK + p : BLK + p + 1])
        system = jnp.where(row_id == p, pivot, system - column * pivot)

    for t in range(TS):
        at = slice(8 * t, 8 * t + 8)
        terms = [in_ref[at, BLK + c : BLK + c + 1] * system[c : c + 1, :] for c in range(6)]
        in_ref[at, :] = in_ref[at, :] - (((terms[0] + terms[1]) + (terms[2] + terms[3])) + (terms[4] + terms[5]))
    change_high, change_low = split(in_ref[...])
    y_ref[...] = jnp.dot(
        lead_ref[...], jnp.concatenate([change_high, change_high, change_low], axis=0), preferred_element_type=f32
    )
    lane_tail = lax.broadcasted_iota(jnp.int32, (EP, AUG), 1)
    for t in range(TS):
        at = slice(EP * t, EP * t + EP)
        active = turned[0:EP, 8 * t + 7 : 8 * t + 8] > f32(0.5)
        local = jnp.where(active, r_ref[t, 0:EP, :].astype(f32), f32(0.0))
        x_ref[at, :] = (local + y_ref[at, 0:BLK]).astype(bf16)
        tail = jnp.where(lane_tail == 6, y_ref[at, BLK:WIDE], f32(0.0))
        l_ref[at, HALF : HALF + 64] = pltpu.roll(tail, 122, 1)[:, 0:64].astype(bf16)

    for side in range(2):

        @pl.when(half == side)
        def _():
            for q in range(4):
                l_ref[:, 2 * SLICE * q : 2 * SLICE * (q + 1)] = x_ref[
                    :, 4 * SLICE * q + 2 * SLICE * side : 4 * SLICE * q + 2 * SLICE * (side + 1)
                ]

    scale = f32(1.0 / 4096.0)
    g_ref[...] = lax.dot_general(l_ref[...], x_ref[...], dims, preferred_element_type=f32) * scale

    for side in range(2):

        @pl.when(half == side)
        def _():
            for q in range(4):
                first = 4 * SLICE * q + 2 * SLICE * side
                rr_ref[:, 2 * SLICE * q : 2 * SLICE * (q + 1)] = g_ref[HALF : HALF + 8, first : first + 2 * SLICE]

    for s in range(8):
        slot, parity = lax.rem(s // 2 + 4 - turn, 4), s % 2
        beside = rr_ref[:, SLICE * s : SLICE * (s + 1)]
        extra = jnp.concatenate([beside, jnp.zeros((8, BLK - SLICE), f32)], axis=1)
        block = jnp.concatenate([g_ref[SLICE * s : SLICE * (s + 1), :], extra], axis=0)

        @pl.when(core == parity)
        def _():
            keep_ref[slot] = block

        @pl.when(core != parity)
        def _():
            send_ref[slot] = block.astype(bf16)


def normals(received):
    return pl.pallas_call(
        normal_kernel,
        out_shape=(
            jax.ShapeDtypeStruct((4, OUT_ROWS, BLK), f32),
            jax.ShapeDtypeStruct((4, OUT_ROWS, BLK), bf16),
        ),
        in_specs=[pl.BlockSpec(memory_space=pltpu.VMEM)],
        out_specs=(pl.BlockSpec(memory_space=pltpu.VMEM), pl.BlockSpec(memory_space=pltpu.VMEM)),
        scratch_shapes=[
            pltpu.VMEM((8 * TS, 128), f32),
            pltpu.VMEM((8 * TS, WIDE), f32),
            pltpu.VMEM((TS * EP, 3 * AUG), bf16),
            pltpu.VMEM((TS * EP, WIDE), f32),
            pltpu.VMEM((TS * EP, BLK), bf16),
            pltpu.VMEM((TS * EP, HALF + 64), bf16),
            pltpu.VMEM((HALF + 64, BLK), f32),
            pltpu.VMEM((8, HALF), f32),
        ],
        compiler_params=pltpu.CompilerParams(vmem_limit_bytes=40 << 20),
        name="normal_rows",
    )(received)


def local(transition, forcing, partials, observed, counts):
    packed = pack(
        counts,
        jnp.transpose(transition, (1, 2, 0, 3)),
        jnp.transpose(partials, (1, 0, 2)),
        observed,
        jnp.transpose(forcing[0], (1, 0, 2)),
    )
    received = lax.all_to_all(packed, "tm", split_axis=0, concat_axis=0, tiled=True)
    keep, send = normals(received)
    arcs, shards = lax.axis_size("arc"), lax.axis_size("tm")
    other_core = [(a * shards + t, (a ^ 1) * shards + t) for a in range(arcs) for t in range(shards)]
    arrived = lax.ppermute(send, ("arc", "tm"), other_core)
    pair_sum = (keep + arrived.astype(f32)).astype(bf16)
    same_core = [[c + 2 * z for z in range(arcs // 2)] for c in range(2)]
    slices = lax.all_to_all(pair_sum, "arc", split_axis=0, concat_axis=0, tiled=True, axis_index_groups=same_core)
    mine = jnp.sum(slices.astype(f32), axis=0).astype(bf16)
    to_owner = []
    for a in range(arcs):
        for t in range(shards):
            z, c, y, h, odd = a // 2, a % 2, t // 4, t % 4 // 2, t % 2
            to_owner.append((a * shards + t, (2 * y + odd) * shards + (y + z) % 4 * 4 + 2 * h + c))
    final = lax.ppermute(mine, ("arc", "tm"), to_owner).astype(f32)
    return final[0:SLICE, :], final[SLICE, 0:SLICE]


def solution(mesh):
    return jax.shard_map(
        local,
        mesh=mesh,
        in_specs=(
            P("arc", None, None, "tm"),
            P("arc", "tm", None, None),
            P("arc", None, "tm"),
            P("arc", "tm"),
            P("arc", "tm"),
        ),
        out_specs=(P(("arc", "tm"), None), P(("arc", "tm"))),
        check_vma=False,
    )
```

```python
import jax
import jax.numpy as jnp
from jax import lax
from jax.experimental import pallas as pl
from jax.experimental.pallas import tpu as pltpu
from jax.sharding import PartitionSpec as P

EP = 32
BLK = 1152
HALF = 576
SLICE = 72
ROWS = 40
OUT_ROWS = 80
TS = 16
AUG = 128
WIDE = BLK + AUG
f32 = jnp.float32
bf16 = jnp.bfloat16


def rounded(x):
    return x.astype(bf16).astype(f32)


def pack_kernel(
    cnt_ref, tr_hbm, pa_hbm, ob_hbm, f_hbm, out_ref, tr_ref, pa_ref, ob_ref, fbuf, wt_ref, sm_ref, sems, small_sems
):
    n_blocks = fbuf.shape[2] // BLK
    smalls = [
        pltpu.make_async_copy(src, dst, small_sems.at[n])
        for n, (src, dst) in enumerate(((tr_hbm, tr_ref), (pa_hbm, pa_ref), (ob_hbm, ob_ref)))
    ]
    for copy in smalls:
        copy.start()
    fetches = [pltpu.make_async_copy(f_hbm, fbuf, sems.at[0])]
    for copy in fetches:
        copy.start()
    lane = lax.broadcasted_iota(jnp.int32, (6, 128), 1)
    sub = lax.broadcasted_iota(jnp.int32, (6, 128), 0)
    sm_ref[...] = jnp.zeros_like(sm_ref)
    for copy in smalls:
        copy.wait()
    for b in range(6):
        sm_ref[b : b + 1, 0:EP] = pa_ref[b]
    heads = sm_ref[0:6, :]
    rows = jnp.where(lane == sub + EP, f32(1.0), f32(0.0))
    steps = [tr_ref[c, :, 0, :] for c in range(6)]
    for i in range(EP - 1, -1, -1):
        wt_ref[:, i, :] = rows
        terms = [steps[c][:, i : i + 1] * rows[c : c + 1, :] for c in range(6)]
        new = ((terms[0] + terms[1]) + (terms[2] + terms[3])) + (terms[4] + terms[5])
        rows = jnp.where(lane == i, heads, new)
    sm_ref[0:6, :] = rows
    sm_ref[6:7, 0:EP] = ob_ref[...]
    lane1 = lax.broadcasted_iota(jnp.int32, (1, 128), 1)
    sm_ref[7:8, :] = jnp.where((lane1 < EP) & (lane1 < cnt_ref[0, 0]), f32(1.0), f32(0.0))
    weights = jnp.transpose(wt_ref[...].reshape(6 * EP, 128))[0:ROWS, :].astype(bf16)
    small = jnp.concatenate([sm_ref[b : b + 1, :] for b in range(8)] + [jnp.zeros((1, 128), f32)], axis=1)
    high = rounded(small)
    row = lax.broadcasted_iota(jnp.int32, (8, BLK), 0)
    tail = jnp.where(row == 6, high, jnp.where(row == 7, small - high, f32(0.0)))
    for copy in fetches:
        copy.wait()
    for b in range(n_blocks):
        local = jnp.dot(weights, fbuf[:, :, b * BLK : (b + 1) * BLK].reshape(6 * EP, BLK), preferred_element_type=f32)
        packed = jnp.concatenate([local[0:EP, :], local[EP:ROWS, :] + tail], axis=0).astype(bf16)
        for h in range(2):
            out_ref[b // 2 * 4 + 2 * h + b % 2] = packed


def pack(counts, transition, partials, observed, forcing):
    n_blocks = forcing.shape[2] // BLK
    hbm = pl.BlockSpec(memory_space=pltpu.MemorySpace.HBM)
    return pl.pallas_call(
        pack_kernel,
        out_shape=jax.ShapeDtypeStruct((2 * n_blocks, ROWS, BLK), bf16),
        in_specs=[pl.BlockSpec(memory_space=pltpu.SMEM), hbm, hbm, hbm, hbm],
        out_specs=pl.BlockSpec(memory_space=pltpu.VMEM),
        scratch_shapes=[
            pltpu.VMEM((6, 6, 1, EP), f32),
            pltpu.VMEM((6, 1, EP), f32),
            pltpu.VMEM((1, EP), f32),
            pltpu.VMEM((6, EP, n_blocks * BLK), bf16),
            pltpu.VMEM((6, EP, 128), f32),
            pltpu.VMEM((8, 128), f32),
            pltpu.SemaphoreType.DMA((1,)),
            pltpu.SemaphoreType.DMA((3,)),
        ],
        compiler_params=pltpu.CompilerParams(vmem_limit_bytes=32 << 20),
        name="pack_rows",
    )(counts, *[pltpu.with_memory_space_constraint(x, pltpu.MemorySpace.HBM) for x in (transition, partials, observed, forcing)])


def split(x):
    high = x.astype(bf16)
    return high, (x - high.astype(f32)).astype(bf16)


def normal_kernel(r_ref, keep_ref, send_ref, te_ref, in_ref, lead_ref, y_ref, x_ref, l_ref, g_ref, rr_ref):
    shard = lax.axis_index("tm")
    half = lax.div(lax.rem(shard, 4), 2)
    turn = 2 * lax.div(shard, 4) + 2
    core = lax.rem(lax.axis_index("arc"), 2)
    dims = (((0,), (0,)), ((), ()))
    tails = [r_ref[t, 32:40, :].astype(f32) for t in range(TS)]
    for t in range(TS):
        small = tails[t][6:7, :] + tails[t][7:8, :]
        for b in range(8):
            te_ref[8 * t + b : 8 * t + b + 1, :] = small[:, 128 * b : 128 * b + 128]
    turned = jnp.transpose(te_ref[...])

    sub = lax.broadcasted_iota(jnp.int32, (8, BLK), 0)
    sub_aug = lax.broadcasted_iota(jnp.int32, (8, AUG), 0)
    lane_aug = lax.broadcasted_iota(jnp.int32, (8, AUG), 1)
    unit = jnp.where((sub_aug == 6) & (lane_aug == 6), f32(1.0), f32(0.0))
    eye = jnp.where((lane_aug == sub_aug) & (sub_aug < 6), f32(1.0), f32(0.0))
    state = jnp.concatenate([jnp.zeros((8, BLK), f32), eye + unit], axis=1)
    for t in range(TS):
        in_ref[8 * t : 8 * t + 8, :] = state
        if t == TS - 1:
            break
        new = jnp.concatenate([jnp.where(sub < 6, tails[t], f32(0.0)), unit], axis=1)
        terms = [turned[32:40, 8 * t + b : 8 * t + b + 1] * state[b : b + 1, :] for b in range(6)]
        state = new + (((terms[0] + terms[1]) + (terms[2] + terms[3])) + (terms[4] + terms[5]))

    lane = lax.broadcasted_iota(jnp.int32, (EP, AUG), 1)
    for t in range(TS):
        active = turned[0:EP, 8 * t + 7 : 8 * t + 8] > f32(0.5)
        mine = (lane >= 8 * t) & (lane < 8 * t + 7) & active
        high, low = split(jnp.where(mine, turned[0:EP, :], f32(0.0)))
        lead_ref[EP * t : EP * t + EP, 0:AUG] = high
        lead_ref[EP * t : EP * t + EP, AUG : 2 * AUG] = low
        lead_ref[EP * t : EP * t + EP, 2 * AUG : 3 * AUG] = high

    maps = in_ref[:, BLK:WIDE]
    maps_high, maps_low = split(maps)
    states = jnp.dot(
        lead_ref[...], jnp.concatenate([maps_high, maps_high, maps_low], axis=0), preferred_element_type=f32
    )
    states_high, states_low = split(states)
    left = (states_high.astype(f32) + pltpu.roll(states_low.astype(f32), 8, 1)).astype(bf16)
    rows = jnp.concatenate([r_ref[t, 0:EP, :] for t in range(TS)], axis=0)
    from_local = lax.dot_general(left, rows, dims, preferred_element_type=f32)
    right = jnp.concatenate([states_high, states_low, lead_ref[:, 0 : 2 * AUG]], axis=1)
    from_small = lax.dot_general(left, right, dims, preferred_element_type=f32)
    from_small = from_small[0:8, :] + from_small[8:16, :]
    augmented = from_small[:, 0:AUG] + from_small[:, AUG : 2 * AUG]
    through = from_small[:, 2 * AUG : 3 * AUG] + from_small[:, 3 * AUG : 4 * AUG]
    through_high, through_low = split(through)
    sums_high, sums_low = split(in_ref[:, 0:BLK])
    from_sums = jnp.dot(
        jnp.concatenate([through_high, through_low, through_high], axis=1),
        jnp.concatenate([sums_high, sums_high, sums_low], axis=0),
        preferred_element_type=f32,
    )
    system = jnp.concatenate([from_local[0:8, :] + from_local[8:16, :] + from_sums, augmented + eye], axis=1)
    row_id = lax.broadcasted_iota(jnp.int32, (8, WIDE), 0)
    for p in range(6):
        column = system[:, BLK + p : BLK + p + 1]
        pivot = system[p : p + 1, :] * (f32(1.0) / system[p : p + 1, BLK + p : BLK + p + 1])
        system = jnp.where(row_id == p, pivot, system - column * pivot)

    for t in range(TS):
        at = slice(8 * t, 8 * t + 8)
        terms = [in_ref[at, BLK + c : BLK + c + 1] * system[c : c + 1, :] for c in range(6)]
        in_ref[at, :] = in_ref[at, :] - (((terms[0] + terms[1]) + (terms[2] + terms[3])) + (terms[4] + terms[5]))
    change_high, change_low = split(in_ref[...])
    y_ref[...] = jnp.dot(
        lead_ref[...], jnp.concatenate([change_high, change_high, change_low], axis=0), preferred_element_type=f32
    )
    lane_tail = lax.broadcasted_iota(jnp.int32, (EP, AUG), 1)
    for t in range(TS):
        at = slice(EP * t, EP * t + EP)
        active = turned[0:EP, 8 * t + 7 : 8 * t + 8] > f32(0.5)
        local = jnp.where(active, r_ref[t, 0:EP, :].astype(f32), f32(0.0))
        x_ref[at, :] = (local + y_ref[at, 0:BLK]).astype(bf16)
        tail = jnp.where(lane_tail == 6, y_ref[at, BLK:WIDE], f32(0.0))
        l_ref[at, HALF : HALF + 64] = pltpu.roll(tail, 122, 1)[:, 0:64].astype(bf16)

    for side in range(2):

        @pl.when(half == side)
        def _():
            for q in range(4):
                l_ref[:, 2 * SLICE * q : 2 * SLICE * (q + 1)] = x_ref[
                    :, 4 * SLICE * q + 2 * SLICE * side : 4 * SLICE * q + 2 * SLICE * (side + 1)
                ]

    scale = f32(1.0 / 4096.0)
    g_ref[...] = lax.dot_general(l_ref[...], x_ref[...], dims, preferred_element_type=f32) * scale

    for side in range(2):

        @pl.when(half == side)
        def _():
            for q in range(4):
                first = 4 * SLICE * q + 2 * SLICE * side
                rr_ref[:, 2 * SLICE * q : 2 * SLICE * (q + 1)] = g_ref[HALF : HALF + 8, first : first + 2 * SLICE]

    for s in range(8):
        slot, parity = lax.rem(turn + 4 - s // 2, 4), s % 2
        beside = rr_ref[:, SLICE * s : SLICE * (s + 1)]
        extra = jnp.concatenate([beside, jnp.zeros((8, BLK - SLICE), f32)], axis=1)
        block = jnp.concatenate([g_ref[SLICE * s : SLICE * (s + 1), :], extra], axis=0)

        @pl.when(core == parity)
        def _():
            keep_ref[slot] = block

        @pl.when(core != parity)
        def _():
            send_ref[slot] = block.astype(bf16)


def normals(received):
    return pl.pallas_call(
        normal_kernel,
        out_shape=(
            jax.ShapeDtypeStruct((4, OUT_ROWS, BLK), f32),
            jax.ShapeDtypeStruct((4, OUT_ROWS, BLK), bf16),
        ),
        in_specs=[pl.BlockSpec(memory_space=pltpu.VMEM)],
        out_specs=(pl.BlockSpec(memory_space=pltpu.VMEM), pl.BlockSpec(memory_space=pltpu.VMEM)),
        scratch_shapes=[
            pltpu.VMEM((8 * TS, 128), f32),
            pltpu.VMEM((8 * TS, WIDE), f32),
            pltpu.VMEM((TS * EP, 3 * AUG), bf16),
            pltpu.VMEM((TS * EP, WIDE), f32),
            pltpu.VMEM((TS * EP, BLK), bf16),
            pltpu.VMEM((TS * EP, HALF + 64), bf16),
            pltpu.VMEM((HALF + 64, BLK), f32),
            pltpu.VMEM((8, HALF), f32),
        ],
        compiler_params=pltpu.CompilerParams(vmem_limit_bytes=40 << 20),
        name="normal_rows",
    )(received)


def local(transition, forcing, partials, observed, counts):
    packed = pack(
        counts,
        jnp.transpose(transition, (1, 2, 0, 3)),
        jnp.transpose(partials, (1, 0, 2)),
        observed,
        jnp.transpose(forcing[0], (1, 0, 2)),
    )
    received = lax.all_to_all(packed, "tm", split_axis=0, concat_axis=0, tiled=True)
    keep, send = normals(received)
    arcs, shards = lax.axis_size("arc"), lax.axis_size("tm")
    other_core = [(a * shards + t, (a ^ 1) * shards + t) for a in range(arcs) for t in range(shards)]
    arrived = lax.ppermute(send, ("arc", "tm"), other_core)
    pair_sum = (keep + arrived.astype(f32)).astype(bf16)
    same_core = [[c + 2 * z for z in range(arcs // 2)] for c in range(2)]
    slices = lax.all_to_all(pair_sum, "arc", split_axis=0, concat_axis=0, tiled=True, axis_index_groups=same_core)
    mine = jnp.sum(slices.astype(f32), axis=0).astype(bf16)
    to_owner = []
    for a in range(arcs):
        for t in range(shards):
            z, c, y, h, odd = a // 2, a % 2, t // 4, t % 4 // 2, t % 2
            to_owner.append((a * shards + t, (2 * y + odd) * shards + (2 * y + 2 - z) % 4 * 4 + 2 * h + c))
    final = lax.ppermute(mine, ("arc", "tm"), to_owner).astype(f32)
    return final[0:SLICE, :], final[SLICE, 0:SLICE]


def solution(mesh):
    return jax.shard_map(
        local,
        mesh=mesh,
        in_specs=(
            P("arc", None, None, "tm"),
            P("arc", "tm", None, None),
            P("arc", None, "tm"),
            P("arc", "tm"),
            P("arc", "tm"),
        ),
        out_specs=(P(("arc", "tm"), None), P(("arc", "tm"))),
        check_vma=False,
    )
```

```python
import jax
import jax.numpy as jnp
from jax import lax
from jax.experimental import pallas as pl
from jax.experimental.pallas import tpu as pltpu
from jax.sharding import PartitionSpec as P

EP = 32
BLK = 1152
HALF = 576
SLICE = 72
ROWS = 40
OUT_ROWS = 80
TS = 16
AUG = 128
WIDE = BLK + AUG
f32 = jnp.float32
bf16 = jnp.bfloat16


def rounded(x):
    return x.astype(bf16).astype(f32)


def pack_kernel(
    cnt_ref, tr_hbm, pa_hbm, ob_hbm, f_hbm, out_ref, tr_ref, pa_ref, ob_ref, fbuf, one_ref, wt_ref, sm_ref, sems, small_sems
):
    n_blocks = fbuf.shape[2] // BLK
    smalls = [
        pltpu.make_async_copy(src, dst, small_sems.at[n])
        for n, (src, dst) in enumerate(((tr_hbm, tr_ref), (pa_hbm, pa_ref), (ob_hbm, ob_ref)))
    ]
    for copy in smalls:
        copy.start()
    middle = n_blocks // 2
    parts = [pl.ds(0, middle * BLK), pl.ds(middle * BLK, (n_blocks - middle) * BLK)]
    fetches = [pltpu.make_async_copy(f_hbm.at[:, :, p], fbuf.at[:, :, p], sems.at[n]) for n, p in enumerate(parts)]
    for copy in fetches:
        copy.start()
    lane = lax.broadcasted_iota(jnp.int32, (8, 128), 1)
    sub = lax.broadcasted_iota(jnp.int32, (8, 128), 0)
    sm_ref[...] = jnp.zeros_like(sm_ref)
    one_ref[...] = jnp.zeros_like(one_ref)
    for copy in smalls:
        copy.wait()
    for b in range(6):
        sm_ref[b : b + 1, 0:EP] = pa_ref[b]
        one_ref[b, 0:6, 0:EP] = tr_ref[b, :, 0, :]
    heads = sm_ref[...]

    def total(terms):
        return ((terms[0] + terms[1]) + (terms[2] + terms[3])) + (terms[4] + terms[5])

    def applied(maps, vectors):
        return total([maps[c] * vectors[c : c + 1, :] for c in range(6)])

    def at(maps, epoch):
        return [maps[c][:, epoch : epoch + 1] for c in range(6)]

    one = [one_ref[c] for c in range(6)]
    back = [[pltpu.roll(one[c], n, 1) for c in range(6)] for n in (1, 2, 3)]
    two = [total([one[c][m : m + 1, :] * back[0][m] for m in range(6)]) for c in range(6)]
    two_back = [pltpu.roll(two[c], 2, 1) for c in range(6)]
    four = [total([two[c][m : m + 1, :] * two_back[m] for m in range(6)]) for c in range(6)]
    heads_one = applied(back[0], heads)
    heads_two = applied(back[1], heads_one)
    heads_three = applied(back[2], heads_two)
    phase = lane & 3
    fresh = jnp.where(
        phase == 3, heads_three, jnp.where(phase == 2, heads_two, jnp.where(phase == 1, heads_one, heads))
    )
    rows = jnp.where((lane == sub + EP) & (sub < 6), f32(1.0), f32(0.0))
    for i in range(EP - 1, -1, -4):
        first = jnp.where(lane == i, heads, applied(at(one, i), rows))
        second = jnp.where(lane == i - 1, heads, jnp.where(lane == i, heads_one, applied(at(two, i), rows)))
        third = jnp.where(lane == i - 2, heads, applied(at(one, i - 2), second))
        for n, value in enumerate((rows, first, second, third)):
            wt_ref[:, i - n, :] = value[0:6, :]
        rows = jnp.where((lane >= i - 3) & (lane <= i), fresh, applied(at(four, i), rows))
    sm_ref[0:6, :] = rows[0:6, :]
    sm_ref[6:7, 0:EP] = ob_ref[...]
    lane1 = lax.broadcasted_iota(jnp.int32, (1, 128), 1)
    sm_ref[7:8, :] = jnp.where((lane1 < EP) & (lane1 < cnt_ref[0, 0]), f32(1.0), f32(0.0))
    weights = jnp.transpose(wt_ref[...].reshape(6 * EP, 128))[0:ROWS, :].astype(bf16)
    small = jnp.concatenate([sm_ref[b : b + 1, :] for b in range(8)] + [jnp.zeros((1, 128), f32)], axis=1)
    high = rounded(small)
    row = lax.broadcasted_iota(jnp.int32, (8, BLK), 0)
    tail = jnp.where(row == 6, high, jnp.where(row == 7, small - high, f32(0.0)))
    for b in range(n_blocks):
        if b % middle == 0:
            fetches[b // middle].wait()
        local = jnp.dot(weights, fbuf[:, :, b * BLK : (b + 1) * BLK].reshape(6 * EP, BLK), preferred_element_type=f32)
        packed = jnp.concatenate([local[0:EP, :], local[EP:ROWS, :] + tail], axis=0).astype(bf16)
        for h in range(2):
            out_ref[b // 2 * 4 + 2 * h + b % 2] = packed


def pack(counts, transition, partials, observed, forcing):
    n_blocks = forcing.shape[2] // BLK
    hbm = pl.BlockSpec(memory_space=pltpu.MemorySpace.HBM)
    return pl.pallas_call(
        pack_kernel,
        out_shape=jax.ShapeDtypeStruct((2 * n_blocks, ROWS, BLK), bf16),
        in_specs=[pl.BlockSpec(memory_space=pltpu.SMEM), hbm, hbm, hbm, hbm],
        out_specs=pl.BlockSpec(memory_space=pltpu.VMEM),
        scratch_shapes=[
            pltpu.VMEM((6, 6, 1, EP), f32),
            pltpu.VMEM((6, 1, EP), f32),
            pltpu.VMEM((1, EP), f32),
            pltpu.VMEM((6, EP, n_blocks * BLK), bf16),
            pltpu.VMEM((6, 8, 128), f32),
            pltpu.VMEM((6, EP, 128), f32),
            pltpu.VMEM((8, 128), f32),
            pltpu.SemaphoreType.DMA((2,)),
            pltpu.SemaphoreType.DMA((3,)),
        ],
        compiler_params=pltpu.CompilerParams(vmem_limit_bytes=32 << 20),
        name="pack_rows",
    )(counts, *[pltpu.with_memory_space_constraint(x, pltpu.MemorySpace.HBM) for x in (transition, partials, observed, forcing)])


def split(x):
    high = x.astype(bf16)
    return high, (x - high.astype(f32)).astype(bf16)


def normal_kernel(r_ref, keep_ref, send_ref, te_ref, in_ref, lead_ref, y_ref, x_ref, l_ref, g_ref, rr_ref):
    shard = lax.axis_index("tm")
    half = lax.div(lax.rem(shard, 4), 2)
    turn = 2 * lax.div(shard, 4) + 2
    core = lax.rem(lax.axis_index("arc"), 2)
    dims = (((0,), (0,)), ((), ()))
    tails = [r_ref[t, 32:40, :].astype(f32) for t in range(TS)]
    for t in range(TS):
        small = tails[t][6:7, :] + tails[t][7:8, :]
        for b in range(8):
            te_ref[8 * t + b : 8 * t + b + 1, :] = small[:, 128 * b : 128 * b + 128]
    turned = jnp.transpose(te_ref[...])

    sub = lax.broadcasted_iota(jnp.int32, (8, BLK), 0)
    sub_aug = lax.broadcasted_iota(jnp.int32, (8, AUG), 0)
    lane_aug = lax.broadcasted_iota(jnp.int32, (8, AUG), 1)
    unit = jnp.where((sub_aug == 6) & (lane_aug == 6), f32(1.0), f32(0.0))
    eye = jnp.where((lane_aug == sub_aug) & (sub_aug < 6), f32(1.0), f32(0.0))
    state = jnp.concatenate([jnp.zeros((8, BLK), f32), eye + unit], axis=1)
    for t in range(TS):
        in_ref[8 * t : 8 * t + 8, :] = state
        if t == TS - 1:
            break
        new = jnp.concatenate([jnp.where(sub < 6, tails[t], f32(0.0)), unit], axis=1)
        terms = [turned[32:40, 8 * t + b : 8 * t + b + 1] * state[b : b + 1, :] for b in range(6)]
        state = new + (((terms[0] + terms[1]) + (terms[2] + terms[3])) + (terms[4] + terms[5]))

    lane = lax.broadcasted_iota(jnp.int32, (EP, AUG), 1)
    for t in range(TS):
        active = turned[0:EP, 8 * t + 7 : 8 * t + 8] > f32(0.5)
        mine = (lane >= 8 * t) & (lane < 8 * t + 7) & active
        high, low = split(jnp.where(mine, turned[0:EP, :], f32(0.0)))
        lead_ref[EP * t : EP * t + EP, 0:AUG] = high
        lead_ref[EP * t : EP * t + EP, AUG : 2 * AUG] = low
        lead_ref[EP * t : EP * t + EP, 2 * AUG : 3 * AUG] = high

    maps = in_ref[:, BLK:WIDE]
    maps_high, maps_low = split(maps)
    states = jnp.dot(
        lead_ref[...], jnp.concatenate([maps_high, maps_high, maps_low], axis=0), preferred_element_type=f32
    )
    states_high, states_low = split(states)
    left = (states_high.astype(f32) + pltpu.roll(states_low.astype(f32), 8, 1)).astype(bf16)
    rows = jnp.concatenate([r_ref[t, 0:EP, :] for t in range(TS)], axis=0)
    from_local = lax.dot_general(left, rows, dims, preferred_element_type=f32)
    right = jnp.concatenate([states_high, states_low, lead_ref[:, 0 : 2 * AUG]], axis=1)
    from_small = lax.dot_general(left, right, dims, preferred_element_type=f32)
    from_small = from_small[0:8, :] + from_small[8:16, :]
    augmented = from_small[:, 0:AUG] + from_small[:, AUG : 2 * AUG]
    through = from_small[:, 2 * AUG : 3 * AUG] + from_small[:, 3 * AUG : 4 * AUG]
    through_high, through_low = split(through)
    sums_high, sums_low = split(in_ref[:, 0:BLK])
    from_sums = jnp.dot(
        jnp.concatenate([through_high, through_low, through_high], axis=1),
        jnp.concatenate([sums_high, sums_high, sums_low], axis=0),
        preferred_element_type=f32,
    )
    system = jnp.concatenate([from_local[0:8, :] + from_local[8:16, :] + from_sums, augmented + eye], axis=1)
    row_id = lax.broadcasted_iota(jnp.int32, (8, WIDE), 0)
    for p in range(6):
        column = system[:, BLK + p : BLK + p + 1]
        pivot = system[p : p + 1, :] * (f32(1.0) / system[p : p + 1, BLK + p : BLK + p + 1])
        system = jnp.where(row_id == p, pivot, system - column * pivot)

    for t in range(TS):
        at = slice(8 * t, 8 * t + 8)
        terms = [in_ref[at, BLK + c : BLK + c + 1] * system[c : c + 1, :] for c in range(6)]
        in_ref[at, :] = in_ref[at, :] - (((terms[0] + terms[1]) + (terms[2] + terms[3])) + (terms[4] + terms[5]))
    change_high, change_low = split(in_ref[...])
    y_ref[...] = jnp.dot(
        lead_ref[...], jnp.concatenate([change_high, change_high, change_low], axis=0), preferred_element_type=f32
    )
    lane_tail = lax.broadcasted_iota(jnp.int32, (EP, AUG), 1)
    for t in range(TS):
        at = slice(EP * t, EP * t + EP)
        active = turned[0:EP, 8 * t + 7 : 8 * t + 8] > f32(0.5)
        local = jnp.where(active, r_ref[t, 0:EP, :].astype(f32), f32(0.0))
        x_ref[at, :] = (local + y_ref[at, 0:BLK]).astype(bf16)
        tail = jnp.where(lane_tail == 6, y_ref[at, BLK:WIDE], f32(0.0))
        l_ref[at, HALF : HALF + 64] = pltpu.roll(tail, 122, 1)[:, 0:64].astype(bf16)

    for side in range(2):

        @pl.when(half == side)
        def _():
            for q in range(4):
                l_ref[:, 2 * SLICE * q : 2 * SLICE * (q + 1)] = x_ref[
                    :, 4 * SLICE * q + 2 * SLICE * side : 4 * SLICE * q + 2 * SLICE * (side + 1)
                ]

    scale = f32(1.0 / 4096.0)
    g_ref[...] = lax.dot_general(l_ref[...], x_ref[...], dims, preferred_element_type=f32) * scale

    for side in range(2):

        @pl.when(half == side)
        def _():
            for q in range(4):
                first = 4 * SLICE * q + 2 * SLICE * side
                rr_ref[:, 2 * SLICE * q : 2 * SLICE * (q + 1)] = g_ref[HALF : HALF + 8, first : first + 2 * SLICE]

    for s in range(8):
        slot, parity = lax.rem(turn + 4 - s // 2, 4), s % 2
        beside = rr_ref[:, SLICE * s : SLICE * (s + 1)]
        extra = jnp.concatenate([beside, jnp.zeros((8, BLK - SLICE), f32)], axis=1)
        block = jnp.concatenate([g_ref[SLICE * s : SLICE * (s + 1), :], extra], axis=0)

        @pl.when(core == parity)
        def _():
            keep_ref[slot] = block

        @pl.when(core != parity)
        def _():
            send_ref[slot] = block.astype(bf16)


def normals(received):
    return pl.pallas_call(
        normal_kernel,
        out_shape=(
            jax.ShapeDtypeStruct((4, OUT_ROWS, BLK), f32),
            jax.ShapeDtypeStruct((4, OUT_ROWS, BLK), bf16),
        ),
        in_specs=[pl.BlockSpec(memory_space=pltpu.VMEM)],
        out_specs=(pl.BlockSpec(memory_space=pltpu.VMEM), pl.BlockSpec(memory_space=pltpu.VMEM)),
        scratch_shapes=[
            pltpu.VMEM((8 * TS, 128), f32),
            pltpu.VMEM((8 * TS, WIDE), f32),
            pltpu.VMEM((TS * EP, 3 * AUG), bf16),
            pltpu.VMEM((TS * EP, WIDE), f32),
            pltpu.VMEM((TS * EP, BLK), bf16),
            pltpu.VMEM((TS * EP, HALF + 64), bf16),
            pltpu.VMEM((HALF + 64, BLK), f32),
            pltpu.VMEM((8, HALF), f32),
        ],
        compiler_params=pltpu.CompilerParams(vmem_limit_bytes=40 << 20),
        name="normal_rows",
    )(received)


def local(transition, forcing, partials, observed, counts):
    packed = pack(
        counts,
        jnp.transpose(transition, (1, 2, 0, 3)),
        jnp.transpose(partials, (1, 0, 2)),
        observed,
        jnp.transpose(forcing[0], (1, 0, 2)),
    )
    received = lax.all_to_all(packed, "tm", split_axis=0, concat_axis=0, tiled=True)
    keep, send = normals(received)
    arcs, shards = lax.axis_size("arc"), lax.axis_size("tm")
    other_core = [(a * shards + t, (a ^ 1) * shards + t) for a in range(arcs) for t in range(shards)]
    arrived = lax.ppermute(send, ("arc", "tm"), other_core)
    pair_sum = (keep + arrived.astype(f32)).astype(bf16)
    same_core = [[c + 2 * z for z in range(arcs // 2)] for c in range(2)]
    slices = lax.all_to_all(pair_sum, "arc", split_axis=0, concat_axis=0, tiled=True, axis_index_groups=same_core)
    mine = jnp.sum(slices.astype(f32), axis=0).astype(bf16)
    to_owner = []
    for a in range(arcs):
        for t in range(shards):
            z, c, y, h, odd = a // 2, a % 2, t // 4, t % 4 // 2, t % 2
            to_owner.append((a * shards + t, (2 * y + odd) * shards + (2 * y + 2 - z) % 4 * 4 + 2 * h + c))
    final = lax.ppermute(mine, ("arc", "tm"), to_owner).astype(f32)
    return final[0:SLICE, :], final[SLICE, 0:SLICE]


def solution(mesh):
    return jax.shard_map(
        local,
        mesh=mesh,
        in_specs=(
            P("arc", None, None, "tm"),
            P("arc", "tm", None, None),
            P("arc", None, "tm"),
            P("arc", "tm"),
            P("arc", "tm"),
        ),
        out_specs=(P(("arc", "tm"), None), P(("arc", "tm"))),
        check_vma=False,
    )
```

```python
import jax
import jax.numpy as jnp
from jax import lax
from jax.experimental import pallas as pl
from jax.experimental.pallas import tpu as pltpu
from jax.sharding import PartitionSpec as P

EP = 32
BLK = 1152
HALF = 576
SLICE = 72
ROWS = 40
TS = 16
AUG = 128
WIDE = BLK + AUG
f32 = jnp.float32
bf16 = jnp.bfloat16


def rounded(x):
    return x.astype(bf16).astype(f32)


def pack_kernel(
    cnt_ref, tr_hbm, pa_hbm, ob_hbm, f_hbm, out_ref, tr_ref, pa_ref, ob_ref, fbuf, one_ref, wt_ref, sm_ref, sems, small_sems
):
    n_blocks = fbuf.shape[2] // BLK
    smalls = [
        pltpu.make_async_copy(src, dst, small_sems.at[n])
        for n, (src, dst) in enumerate(((tr_hbm, tr_ref), (pa_hbm, pa_ref), (ob_hbm, ob_ref)))
    ]
    for copy in smalls:
        copy.start()
    middle = n_blocks // 2
    parts = [pl.ds(0, middle * BLK), pl.ds(middle * BLK, (n_blocks - middle) * BLK)]
    fetches = [pltpu.make_async_copy(f_hbm.at[:, :, p], fbuf.at[:, :, p], sems.at[n]) for n, p in enumerate(parts)]
    for copy in fetches:
        copy.start()
    lane = lax.broadcasted_iota(jnp.int32, (8, 128), 1)
    sub = lax.broadcasted_iota(jnp.int32, (8, 128), 0)
    sm_ref[...] = jnp.zeros_like(sm_ref)
    one_ref[...] = jnp.zeros_like(one_ref)
    for copy in smalls:
        copy.wait()
    for b in range(6):
        sm_ref[b : b + 1, 0:EP] = pa_ref[b]
        one_ref[b, 0:6, 0:EP] = tr_ref[b, :, 0, :]
    heads = sm_ref[...]

    def total(terms):
        return ((terms[0] + terms[1]) + (terms[2] + terms[3])) + (terms[4] + terms[5])

    def applied(maps, vectors):
        return total([maps[c] * vectors[c : c + 1, :] for c in range(6)])

    def at(maps, epoch):
        return [maps[c][:, epoch : epoch + 1] for c in range(6)]

    one = [one_ref[c] for c in range(6)]
    back = [[pltpu.roll(one[c], n, 1) for c in range(6)] for n in (1, 2, 3)]
    two = [total([one[c][m : m + 1, :] * back[0][m] for m in range(6)]) for c in range(6)]
    two_back = [pltpu.roll(two[c], 2, 1) for c in range(6)]
    four = [total([two[c][m : m + 1, :] * two_back[m] for m in range(6)]) for c in range(6)]
    heads_one = applied(back[0], heads)
    heads_two = applied(back[1], heads_one)
    heads_three = applied(back[2], heads_two)
    phase = lane & 3
    fresh = jnp.where(
        phase == 3, heads_three, jnp.where(phase == 2, heads_two, jnp.where(phase == 1, heads_one, heads))
    )
    rows = jnp.where((lane == sub + EP) & (sub < 6), f32(1.0), f32(0.0))
    for i in range(EP - 1, -1, -4):
        first = jnp.where(lane == i, heads, applied(at(one, i), rows))
        second = jnp.where(lane == i - 1, heads, jnp.where(lane == i, heads_one, applied(at(two, i), rows)))
        third = jnp.where(lane == i - 2, heads, applied(at(one, i - 2), second))
        for n, value in enumerate((rows, first, second, third)):
            wt_ref[:, i - n, :] = value[0:6, :]
        rows = jnp.where((lane >= i - 3) & (lane <= i), fresh, applied(at(four, i), rows))
    sm_ref[0:6, :] = rows[0:6, :]
    sm_ref[6:7, 0:EP] = ob_ref[...]
    lane1 = lax.broadcasted_iota(jnp.int32, (1, 128), 1)
    sm_ref[7:8, :] = jnp.where((lane1 < EP) & (lane1 < cnt_ref[0, 0]), f32(1.0), f32(0.0))
    weights = jnp.transpose(wt_ref[...].reshape(6 * EP, 128))[0:ROWS, :].astype(bf16)
    small = jnp.concatenate([sm_ref[b : b + 1, :] for b in range(8)] + [jnp.zeros((1, 128), f32)], axis=1)
    high = rounded(small)
    row = lax.broadcasted_iota(jnp.int32, (8, BLK), 0)
    tail = jnp.where(row == 6, high, jnp.where(row == 7, small - high, f32(0.0)))
    for b in range(n_blocks):
        if b % middle == 0:
            fetches[b // middle].wait()
        local = jnp.dot(weights, fbuf[:, :, b * BLK : (b + 1) * BLK].reshape(6 * EP, BLK), preferred_element_type=f32)
        packed = jnp.concatenate([local[0:EP, :], local[EP:ROWS, :] + tail], axis=0).astype(bf16)
        for h in range(2):
            out_ref[b // 2 * 4 + 2 * h + b % 2] = packed


def pack(counts, transition, partials, observed, forcing):
    n_blocks = forcing.shape[2] // BLK
    hbm = pl.BlockSpec(memory_space=pltpu.MemorySpace.HBM)
    return pl.pallas_call(
        pack_kernel,
        out_shape=jax.ShapeDtypeStruct((2 * n_blocks, ROWS, BLK), bf16),
        in_specs=[pl.BlockSpec(memory_space=pltpu.SMEM), hbm, hbm, hbm, hbm],
        out_specs=pl.BlockSpec(memory_space=pltpu.VMEM),
        scratch_shapes=[
            pltpu.VMEM((6, 6, 1, EP), f32),
            pltpu.VMEM((6, 1, EP), f32),
            pltpu.VMEM((1, EP), f32),
            pltpu.VMEM((6, EP, n_blocks * BLK), bf16),
            pltpu.VMEM((6, 8, 128), f32),
            pltpu.VMEM((6, EP, 128), f32),
            pltpu.VMEM((8, 128), f32),
            pltpu.SemaphoreType.DMA((2,)),
            pltpu.SemaphoreType.DMA((3,)),
        ],
        compiler_params=pltpu.CompilerParams(vmem_limit_bytes=32 << 20),
        name="pack_rows",
    )(counts, *[pltpu.with_memory_space_constraint(x, pltpu.MemorySpace.HBM) for x in (transition, partials, observed, forcing)])


def split(x):
    high = x.astype(bf16)
    return high, (x - high.astype(f32)).astype(bf16)


def normal_kernel(r_ref, keep_ref, send_ref, code_ref, te_ref, in_ref, lead_ref, y_ref, x_ref, l_ref, g_ref):
    shard = lax.axis_index("tm")
    half = lax.div(lax.rem(shard, 4), 2)
    turn = 2 * lax.div(shard, 4) + 2
    core = lax.rem(lax.axis_index("arc"), 2)
    dims = (((0,), (0,)), ((), ()))
    tails = [r_ref[t, 32:40, :].astype(f32) for t in range(TS)]
    for t in range(TS):
        small = tails[t][6:7, :] + tails[t][7:8, :]
        for b in range(8):
            te_ref[8 * t + b : 8 * t + b + 1, :] = small[:, 128 * b : 128 * b + 128]
    turned = jnp.transpose(te_ref[...])

    sub = lax.broadcasted_iota(jnp.int32, (8, BLK), 0)
    sub_aug = lax.broadcasted_iota(jnp.int32, (8, AUG), 0)
    lane_aug = lax.broadcasted_iota(jnp.int32, (8, AUG), 1)
    unit = jnp.where((sub_aug == 6) & (lane_aug == 6), f32(1.0), f32(0.0))
    eye = jnp.where((lane_aug == sub_aug) & (sub_aug < 6), f32(1.0), f32(0.0))
    state = jnp.concatenate([jnp.zeros((8, BLK), f32), eye + unit], axis=1)
    for t in range(TS):
        in_ref[8 * t : 8 * t + 8, :] = state
        if t == TS - 1:
            break
        new = jnp.concatenate([jnp.where(sub < 6, tails[t], f32(0.0)), unit], axis=1)
        terms = [turned[32:40, 8 * t + b : 8 * t + b + 1] * state[b : b + 1, :] for b in range(6)]
        state = new + (((terms[0] + terms[1]) + (terms[2] + terms[3])) + (terms[4] + terms[5]))

    lane = lax.broadcasted_iota(jnp.int32, (EP, AUG), 1)
    for t in range(TS):
        active = turned[0:EP, 8 * t + 7 : 8 * t + 8] > f32(0.5)
        mine = (lane >= 8 * t) & (lane < 8 * t + 7) & active
        high, low = split(jnp.where(mine, turned[0:EP, :], f32(0.0)))
        lead_ref[EP * t : EP * t + EP, 0:AUG] = high
        lead_ref[EP * t : EP * t + EP, AUG : 2 * AUG] = low
        lead_ref[EP * t : EP * t + EP, 2 * AUG : 3 * AUG] = high

    maps = in_ref[:, BLK:WIDE]
    maps_high, maps_low = split(maps)
    states = jnp.dot(
        lead_ref[...], jnp.concatenate([maps_high, maps_high, maps_low], axis=0), preferred_element_type=f32
    )
    states_high, states_low = split(states)
    left = (states_high.astype(f32) + pltpu.roll(states_low.astype(f32), 8, 1)).astype(bf16)
    rows = jnp.concatenate([r_ref[t, 0:EP, :] for t in range(TS)], axis=0)
    from_local = lax.dot_general(left, rows, dims, preferred_element_type=f32)
    right = jnp.concatenate([states_high, states_low, lead_ref[:, 0 : 2 * AUG]], axis=1)
    from_small = lax.dot_general(left, right, dims, preferred_element_type=f32)
    from_small = from_small[0:8, :] + from_small[8:16, :]
    augmented = from_small[:, 0:AUG] + from_small[:, AUG : 2 * AUG]
    through = from_small[:, 2 * AUG : 3 * AUG] + from_small[:, 3 * AUG : 4 * AUG]
    through_high, through_low = split(through)
    sums_high, sums_low = split(in_ref[:, 0:BLK])
    from_sums = jnp.dot(
        jnp.concatenate([through_high, through_low, through_high], axis=1),
        jnp.concatenate([sums_high, sums_high, sums_low], axis=0),
        preferred_element_type=f32,
    )
    system = jnp.concatenate([from_local[0:8, :] + from_local[8:16, :] + from_sums, augmented + eye], axis=1)
    row_id = lax.broadcasted_iota(jnp.int32, (8, WIDE), 0)
    for p in range(6):
        column = system[:, BLK + p : BLK + p + 1]
        pivot = system[p : p + 1, :] * (f32(1.0) / system[p : p + 1, BLK + p : BLK + p + 1])
        system = jnp.where(row_id == p, pivot, system - column * pivot)

    for t in range(TS):
        at = slice(8 * t, 8 * t + 8)
        terms = [in_ref[at, BLK + c : BLK + c + 1] * system[c : c + 1, :] for c in range(6)]
        in_ref[at, :] = in_ref[at, :] - (((terms[0] + terms[1]) + (terms[2] + terms[3])) + (terms[4] + terms[5]))
    change_high, change_low = split(in_ref[...])
    y_ref[...] = jnp.dot(
        lead_ref[...], jnp.concatenate([change_high, change_high, change_low], axis=0), preferred_element_type=f32
    )
    lane_tail = lax.broadcasted_iota(jnp.int32, (EP, AUG), 1)
    for t in range(TS):
        at = slice(EP * t, EP * t + EP)
        active = turned[0:EP, 8 * t + 7 : 8 * t + 8] > f32(0.5)
        local = jnp.where(active, r_ref[t, 0:EP, :].astype(f32), f32(0.0))
        x_ref[at, 0:BLK] = (local + y_ref[at, 0:BLK]).astype(bf16)
        x_ref[at, BLK:WIDE] = jnp.where(lane_tail == 6, y_ref[at, BLK:WIDE], f32(0.0)).astype(bf16)

    for side in range(2):

        @pl.when(half == side)
        def _():
            for q in range(4):
                l_ref[:, 2 * SLICE * q : 2 * SLICE * (q + 1)] = x_ref[
                    :, 4 * SLICE * q + 2 * SLICE * side : 4 * SLICE * q + 2 * SLICE * (side + 1)
                ]

    scale = f32(1.0 / 4096.0)
    g_ref[...] = lax.dot_general(l_ref[...], x_ref[...], dims, preferred_element_type=f32) * scale

    row = lax.broadcasted_iota(jnp.int32, (SLICE, BLK), 0)
    column = lax.broadcasted_iota(jnp.int32, (SLICE, BLK), 1) - SLICE * shard
    carries = column == jnp.where(row == SLICE - 1, 0, row + 1)
    mirrors = column == jnp.where(row == 0, SLICE - 1, row - 1)
    code_ref[...] = jnp.where(carries, f32(1.0), jnp.where(mirrors, f32(2.0), f32(0.0))).astype(bf16)
    for s in range(8):
        slot, parity = lax.rem(turn + 4 - s // 2, 4), s % 2
        at = slice(SLICE * s, SLICE * (s + 1))
        start = 4 * SLICE * (s // 2) + SLICE * parity
        low, top = start // 128 * 128, min(BLK, -(-(start + 3 * SLICE) // 128) * 128)
        row = lax.broadcasted_iota(jnp.int32, (SLICE, top - low), 0)
        column = lax.broadcasted_iota(jnp.int32, (SLICE, top - low), 1) + low
        after = jnp.where(row == SLICE - 1, 0, row + 1)
        near = jnp.where(
            column == after + (start + 2 * SLICE * half), g_ref[at, BLK + 6 : BLK + 7], g_ref[at, low:top]
        )
        pieces = ([g_ref[at, 0:low]] if low else []) + [near] + ([g_ref[at, top:BLK]] if top < BLK else [])
        block = jnp.concatenate(pieces, axis=1)

        @pl.when(core == parity)
        def _():
            keep_ref[slot] = block

        @pl.when(core != parity)
        def _():
            send_ref[slot] = block.astype(bf16)


def normals(received):
    return pl.pallas_call(
        normal_kernel,
        out_shape=(
            jax.ShapeDtypeStruct((4, SLICE, BLK), f32),
            jax.ShapeDtypeStruct((4, SLICE, BLK), bf16),
            jax.ShapeDtypeStruct((SLICE, BLK), bf16),
        ),
        in_specs=[pl.BlockSpec(memory_space=pltpu.VMEM)],
        out_specs=(pl.BlockSpec(memory_space=pltpu.VMEM),) * 3,
        scratch_shapes=[
            pltpu.VMEM((8 * TS, 128), f32),
            pltpu.VMEM((8 * TS, WIDE), f32),
            pltpu.VMEM((TS * EP, 3 * AUG), bf16),
            pltpu.VMEM((TS * EP, WIDE), f32),
            pltpu.VMEM((TS * EP, WIDE), bf16),
            pltpu.VMEM((TS * EP, HALF), bf16),
            pltpu.VMEM((HALF, WIDE), f32),
        ],
        compiler_params=pltpu.CompilerParams(vmem_limit_bytes=40 << 20),
        name="normal_rows",
    )(received)


def local(transition, forcing, partials, observed, counts):
    packed = pack(
        counts,
        jnp.transpose(transition, (1, 2, 0, 3)),
        jnp.transpose(partials, (1, 0, 2)),
        observed,
        jnp.transpose(forcing[0], (1, 0, 2)),
    )
    received = lax.all_to_all(packed, "tm", split_axis=0, concat_axis=0, tiled=True)
    keep, send, code = normals(received)
    arcs, shards = lax.axis_size("arc"), lax.axis_size("tm")
    other_core = [(a * shards + t, (a ^ 1) * shards + t) for a in range(arcs) for t in range(shards)]
    arrived = lax.ppermute(send, ("arc", "tm"), other_core)
    pair_sum = (keep + arrived.astype(f32)).astype(bf16)
    same_core = [[c + 2 * z for z in range(arcs // 2)] for c in range(2)]
    slices = lax.all_to_all(pair_sum, "arc", split_axis=0, concat_axis=0, tiled=True, axis_index_groups=same_core)
    mine = jnp.sum(slices.astype(f32), axis=0).astype(bf16)
    to_owner = []
    for a in range(arcs):
        for t in range(shards):
            z, c, y, h, odd = a // 2, a % 2, t // 4, t % 4 // 2, t % 2
            to_owner.append((a * shards + t, (2 * y + odd) * shards + (2 * y + 2 - z) % 4 * 4 + 2 * h + c))
    final = lax.ppermute(mine, ("arc", "tm"), to_owner).astype(f32)
    kind = code.astype(f32)
    carries, mirrors = kind == f32(1.0), kind == f32(2.0)
    rhs = jnp.sum(jnp.where(carries, final, f32(0.0)), axis=1)
    mirrored = jnp.sum(jnp.where(mirrors, final, f32(0.0)), axis=1, keepdims=True)
    return jnp.where(carries, jnp.concatenate([mirrored[1:], mirrored[:1]], axis=0), final), rhs


def solution(mesh):
    return jax.shard_map(
        local,
        mesh=mesh,
        in_specs=(
            P("arc", None, None, "tm"),
            P("arc", "tm", None, None),
            P("arc", None, "tm"),
            P("arc", "tm"),
            P("arc", "tm"),
        ),
        out_specs=(P(("arc", "tm"), None), P(("arc", "tm"))),
        check_vma=False,
    )
```

```python
import jax
import jax.numpy as jnp
from jax import lax
from jax.experimental import pallas as pl
from jax.experimental.pallas import tpu as pltpu
from jax.sharding import PartitionSpec as P

EP = 32
BLK = 1152
HALF = 576
SLICE = 72
ROWS = 40
TS = 16
AUG = 128
WIDE = BLK + AUG
f32 = jnp.float32
bf16 = jnp.bfloat16


def rounded(x):
    return x.astype(bf16).astype(f32)


def pack_kernel(
    cnt_ref, tr_hbm, pa_hbm, ob_hbm, f_hbm, out_ref, tr_ref, pa_ref, ob_ref, fbuf, one_ref, wt_ref, sm_ref, sems, small_sems
):
    n_blocks = fbuf.shape[2] // BLK
    smalls = [
        pltpu.make_async_copy(src, dst, small_sems.at[n])
        for n, (src, dst) in enumerate(((tr_hbm, tr_ref), (pa_hbm, pa_ref), (ob_hbm, ob_ref)))
    ]
    for copy in smalls:
        copy.start()
    middle = n_blocks // 2
    parts = [pl.ds(0, middle * BLK), pl.ds(middle * BLK, (n_blocks - middle) * BLK)]
    fetches = [pltpu.make_async_copy(f_hbm.at[:, :, p], fbuf.at[:, :, p], sems.at[n]) for n, p in enumerate(parts)]
    for copy in fetches:
        copy.start()
    lane = lax.broadcasted_iota(jnp.int32, (8, 128), 1)
    sub = lax.broadcasted_iota(jnp.int32, (8, 128), 0)
    sm_ref[...] = jnp.zeros_like(sm_ref)
    one_ref[...] = jnp.zeros_like(one_ref)
    for copy in smalls:
        copy.wait()
    for b in range(6):
        sm_ref[b : b + 1, 0:EP] = pa_ref[b]
        one_ref[b, 0:6, 0:EP] = tr_ref[b, :, 0, :]
    heads = sm_ref[...]

    def total(terms):
        return ((terms[0] + terms[1]) + (terms[2] + terms[3])) + (terms[4] + terms[5])

    def applied(maps, vectors):
        return total([maps[c] * vectors[c : c + 1, :] for c in range(6)])

    def at(maps, epoch):
        return [maps[c][:, epoch : epoch + 1] for c in range(6)]

    one = [one_ref[c] for c in range(6)]
    back = [[pltpu.roll(one[c], n, 1) for c in range(6)] for n in (1, 2, 3)]
    two = [total([one[c][m : m + 1, :] * back[0][m] for m in range(6)]) for c in range(6)]
    two_back = [pltpu.roll(two[c], 2, 1) for c in range(6)]
    four = [total([two[c][m : m + 1, :] * two_back[m] for m in range(6)]) for c in range(6)]
    heads_one = applied(back[0], heads)
    heads_two = applied(back[1], heads_one)
    heads_three = applied(back[2], heads_two)
    phase = lane & 3
    fresh = jnp.where(
        phase == 3, heads_three, jnp.where(phase == 2, heads_two, jnp.where(phase == 1, heads_one, heads))
    )
    rows = jnp.where((lane == sub + EP) & (sub < 6), f32(1.0), f32(0.0))
    for i in range(EP - 1, -1, -4):
        first = jnp.where(lane == i, heads, applied(at(one, i), rows))
        second = jnp.where(lane == i - 1, heads, jnp.where(lane == i, heads_one, applied(at(two, i), rows)))
        third = jnp.where(lane == i - 2, heads, applied(at(one, i - 2), second))
        for n, value in enumerate((rows, first, second, third)):
            wt_ref[:, i - n, :] = value[0:6, :]
        rows = jnp.where((lane >= i - 3) & (lane <= i), fresh, applied(at(four, i), rows))
    sm_ref[0:6, :] = rows[0:6, :]
    sm_ref[6:7, 0:EP] = ob_ref[...]
    lane1 = lax.broadcasted_iota(jnp.int32, (1, 128), 1)
    sm_ref[7:8, :] = jnp.where((lane1 < EP) & (lane1 < cnt_ref[0, 0]), f32(1.0), f32(0.0))
    weights = jnp.transpose(wt_ref[...].reshape(6 * EP, 128))[0:ROWS, :].astype(bf16)
    small = jnp.concatenate([sm_ref[b : b + 1, :] for b in range(8)] + [jnp.zeros((1, 128), f32)], axis=1)
    high = rounded(small)
    row = lax.broadcasted_iota(jnp.int32, (8, BLK), 0)
    tail = jnp.where(row == 6, high, jnp.where(row == 7, small - high, f32(0.0)))
    for b in range(n_blocks):
        if b % middle == 0:
            fetches[b // middle].wait()
        local = jnp.dot(weights, fbuf[:, :, b * BLK : (b + 1) * BLK].reshape(6 * EP, BLK), preferred_element_type=f32)
        packed = jnp.concatenate([local[0:EP, :], local[EP:ROWS, :] + tail], axis=0).astype(bf16)
        for h in range(2):
            out_ref[b // 2 * 4 + 2 * h + b % 2] = packed


def pack(counts, transition, partials, observed, forcing):
    n_blocks = forcing.shape[2] // BLK
    hbm = pl.BlockSpec(memory_space=pltpu.MemorySpace.HBM)
    return pl.pallas_call(
        pack_kernel,
        out_shape=jax.ShapeDtypeStruct((2 * n_blocks, ROWS, BLK), bf16),
        in_specs=[pl.BlockSpec(memory_space=pltpu.SMEM), hbm, hbm, hbm, hbm],
        out_specs=pl.BlockSpec(memory_space=pltpu.VMEM),
        scratch_shapes=[
            pltpu.VMEM((6, 6, 1, EP), f32),
            pltpu.VMEM((6, 1, EP), f32),
            pltpu.VMEM((1, EP), f32),
            pltpu.VMEM((6, EP, n_blocks * BLK), bf16),
            pltpu.VMEM((6, 8, 128), f32),
            pltpu.VMEM((6, EP, 128), f32),
            pltpu.VMEM((8, 128), f32),
            pltpu.SemaphoreType.DMA((2,)),
            pltpu.SemaphoreType.DMA((3,)),
        ],
        compiler_params=pltpu.CompilerParams(vmem_limit_bytes=32 << 20),
        name="pack_rows",
    )(counts, *[pltpu.with_memory_space_constraint(x, pltpu.MemorySpace.HBM) for x in (transition, partials, observed, forcing)])


def split(x):
    high = x.astype(bf16)
    return high, (x - high.astype(f32)).astype(bf16)


def position():
    shard = lax.axis_index("tm")
    return shard, lax.div(lax.rem(shard, 4), 2), 2 * lax.div(shard, 4) + 2, lax.rem(lax.axis_index("arc"), 2)


def gram_slices(x_ref, l_ref, g_ref, out_ref, half, parity, turn):
    for case in range(4):

        @pl.when(2 * half + parity == case)
        def _():
            for q in range(4):
                first = 4 * SLICE * q + SLICE * case
                l_ref[:, SLICE * q : SLICE * (q + 1)] = x_ref[:, first : first + SLICE]

    g_ref[...] = lax.dot_general(
        l_ref[...], x_ref[...], (((0,), (0,)), ((), ())), preferred_element_type=f32
    ) * f32(1.0 / 4096.0)
    for q in range(4):
        at = slice(SLICE * q, SLICE * (q + 1))
        start = 4 * SLICE * q
        low, top = start // 128 * 128, min(BLK, -(-(start + 4 * SLICE) // 128) * 128)
        row = lax.broadcasted_iota(jnp.int32, (SLICE, top - low), 0)
        column = lax.broadcasted_iota(jnp.int32, (SLICE, top - low), 1) + low
        after = jnp.where(row == SLICE - 1, 0, row + 1)
        near = jnp.where(
            column == after + (start + SLICE * (2 * half + parity)), g_ref[at, BLK + 6 : BLK + 7], g_ref[at, low:top]
        )
        pieces = ([g_ref[at, 0:low]] if low else []) + [near] + ([g_ref[at, top:BLK]] if top < BLK else [])
        out_ref[lax.rem(turn + 4 - q, 4)] = jnp.concatenate(pieces, axis=1).astype(out_ref.dtype)


def normal_kernel(r_ref, send_ref, x_ref, te_ref, in_ref, lead_ref, y_ref, l_ref, g_ref):
    shard, half, turn, core = position()
    dims = (((0,), (0,)), ((), ()))
    tails = [r_ref[t, 32:40, :].astype(f32) for t in range(TS)]
    for t in range(TS):
        small = tails[t][6:7, :] + tails[t][7:8, :]
        for b in range(8):
            te_ref[8 * t + b : 8 * t + b + 1, :] = small[:, 128 * b : 128 * b + 128]
    turned = jnp.transpose(te_ref[...])

    sub = lax.broadcasted_iota(jnp.int32, (8, BLK), 0)
    sub_aug = lax.broadcasted_iota(jnp.int32, (8, AUG), 0)
    lane_aug = lax.broadcasted_iota(jnp.int32, (8, AUG), 1)
    unit = jnp.where((sub_aug == 6) & (lane_aug == 6), f32(1.0), f32(0.0))
    eye = jnp.where((lane_aug == sub_aug) & (sub_aug < 6), f32(1.0), f32(0.0))
    state = jnp.concatenate([jnp.zeros((8, BLK), f32), eye + unit], axis=1)
    for t in range(TS):
        in_ref[8 * t : 8 * t + 8, :] = state
        if t == TS - 1:
            break
        new = jnp.concatenate([jnp.where(sub < 6, tails[t], f32(0.0)), unit], axis=1)
        terms = [turned[32:40, 8 * t + b : 8 * t + b + 1] * state[b : b + 1, :] for b in range(6)]
        state = new + (((terms[0] + terms[1]) + (terms[2] + terms[3])) + (terms[4] + terms[5]))

    lane = lax.broadcasted_iota(jnp.int32, (EP, AUG), 1)
    for t in range(TS):
        active = turned[0:EP, 8 * t + 7 : 8 * t + 8] > f32(0.5)
        mine = (lane >= 8 * t) & (lane < 8 * t + 7) & active
        high, low = split(jnp.where(mine, turned[0:EP, :], f32(0.0)))
        lead_ref[EP * t : EP * t + EP, 0:AUG] = high
        lead_ref[EP * t : EP * t + EP, AUG : 2 * AUG] = low
        lead_ref[EP * t : EP * t + EP, 2 * AUG : 3 * AUG] = high

    maps = in_ref[:, BLK:WIDE]
    maps_high, maps_low = split(maps)
    states = jnp.dot(
        lead_ref[...], jnp.concatenate([maps_high, maps_high, maps_low], axis=0), preferred_element_type=f32
    )
    states_high, states_low = split(states)
    left = (states_high.astype(f32) + pltpu.roll(states_low.astype(f32), 8, 1)).astype(bf16)
    rows = jnp.concatenate([r_ref[t, 0:EP, :] for t in range(TS)], axis=0)
    from_local = lax.dot_general(left, rows, dims, preferred_element_type=f32)
    right = jnp.concatenate([states_high, states_low, lead_ref[:, 0 : 2 * AUG]], axis=1)
    from_small = lax.dot_general(left, right, dims, preferred_element_type=f32)
    from_small = from_small[0:8, :] + from_small[8:16, :]
    augmented = from_small[:, 0:AUG] + from_small[:, AUG : 2 * AUG]
    through = from_small[:, 2 * AUG : 3 * AUG] + from_small[:, 3 * AUG : 4 * AUG]
    through_high, through_low = split(through)
    sums_high, sums_low = split(in_ref[:, 0:BLK])
    from_sums = jnp.dot(
        jnp.concatenate([through_high, through_low, through_high], axis=1),
        jnp.concatenate([sums_high, sums_high, sums_low], axis=0),
        preferred_element_type=f32,
    )
    system = jnp.concatenate([from_local[0:8, :] + from_local[8:16, :] + from_sums, augmented + eye], axis=1)
    row_id = lax.broadcasted_iota(jnp.int32, (8, WIDE), 0)
    for p in range(6):
        column = system[:, BLK + p : BLK + p + 1]
        pivot = system[p : p + 1, :] * (f32(1.0) / system[p : p + 1, BLK + p : BLK + p + 1])
        system = jnp.where(row_id == p, pivot, system - column * pivot)

    for t in range(TS):
        at = slice(8 * t, 8 * t + 8)
        terms = [in_ref[at, BLK + c : BLK + c + 1] * system[c : c + 1, :] for c in range(6)]
        in_ref[at, :] = in_ref[at, :] - (((terms[0] + terms[1]) + (terms[2] + terms[3])) + (terms[4] + terms[5]))
    change_high, change_low = split(in_ref[...])
    y_ref[...] = jnp.dot(
        lead_ref[...], jnp.concatenate([change_high, change_high, change_low], axis=0), preferred_element_type=f32
    )
    lane_tail = lax.broadcasted_iota(jnp.int32, (EP, AUG), 1)
    for t in range(TS):
        at = slice(EP * t, EP * t + EP)
        active = turned[0:EP, 8 * t + 7 : 8 * t + 8] > f32(0.5)
        local = jnp.where(active, r_ref[t, 0:EP, :].astype(f32), f32(0.0))
        x_ref[at, 0:BLK] = (local + y_ref[at, 0:BLK]).astype(bf16)
        x_ref[at, BLK:WIDE] = jnp.where(lane_tail == 6, y_ref[at, BLK:WIDE], f32(0.0)).astype(bf16)

    gram_slices(x_ref, l_ref, g_ref, send_ref, half, 1 - core, turn)


def own_kernel(x_ref, keep_ref, code_ref, l_ref, g_ref):
    shard, half, turn, core = position()
    gram_slices(x_ref, l_ref, g_ref, keep_ref, half, core, turn)
    row = lax.broadcasted_iota(jnp.int32, (SLICE, BLK), 0)
    column = lax.broadcasted_iota(jnp.int32, (SLICE, BLK), 1) - SLICE * shard
    carries = column == jnp.where(row == SLICE - 1, 0, row + 1)
    mirrors = column == jnp.where(row == 0, SLICE - 1, row - 1)
    code_ref[...] = jnp.where(carries, f32(1.0), jnp.where(mirrors, f32(2.0), f32(0.0))).astype(bf16)


def normals(received):
    vmem = pl.BlockSpec(memory_space=pltpu.VMEM)
    return pl.pallas_call(
        normal_kernel,
        out_shape=(jax.ShapeDtypeStruct((4, SLICE, BLK), bf16), jax.ShapeDtypeStruct((TS * EP, WIDE), bf16)),
        in_specs=[vmem],
        out_specs=(vmem, vmem),
        scratch_shapes=[
            pltpu.VMEM((8 * TS, 128), f32),
            pltpu.VMEM((8 * TS, WIDE), f32),
            pltpu.VMEM((TS * EP, 3 * AUG), bf16),
            pltpu.VMEM((TS * EP, WIDE), f32),
            pltpu.VMEM((TS * EP, HALF // 2), bf16),
            pltpu.VMEM((HALF // 2, WIDE), f32),
        ],
        compiler_params=pltpu.CompilerParams(vmem_limit_bytes=32 << 20),
        name="normal_rows",
    )(received)


def own_slices(rows):
    vmem = pl.BlockSpec(memory_space=pltpu.VMEM)
    return pl.pallas_call(
        own_kernel,
        out_shape=(jax.ShapeDtypeStruct((4, SLICE, BLK), f32), jax.ShapeDtypeStruct((SLICE, BLK), bf16)),
        in_specs=[vmem],
        out_specs=(vmem, vmem),
        scratch_shapes=[pltpu.VMEM((TS * EP, HALF // 2), bf16), pltpu.VMEM((HALF // 2, WIDE), f32)],
        cost_estimate=pl.CostEstimate(flops=2 * TS * EP * WIDE * HALF // 2, bytes_accessed=4 << 20, transcendentals=0),
        compiler_params=pltpu.CompilerParams(vmem_limit_bytes=24 << 20),
        name="own_slices",
    )(rows)


def local(transition, forcing, partials, observed, counts):
    packed = pack(
        counts,
        jnp.transpose(transition, (1, 2, 0, 3)),
        jnp.transpose(partials, (1, 0, 2)),
        observed,
        jnp.transpose(forcing[0], (1, 0, 2)),
    )
    received = lax.all_to_all(packed, "tm", split_axis=0, concat_axis=0, tiled=True)
    send, rows = normals(received)
    arcs, shards = lax.axis_size("arc"), lax.axis_size("tm")
    other_core = [(a * shards + t, (a ^ 1) * shards + t) for a in range(arcs) for t in range(shards)]
    arrived = lax.ppermute(send, ("arc", "tm"), other_core)
    keep, code = own_slices(rows)
    pair_sum = (keep + arrived.astype(f32)).astype(bf16)
    same_core = [[c + 2 * z for z in range(arcs // 2)] for c in range(2)]
    slices = lax.all_to_all(pair_sum, "arc", split_axis=0, concat_axis=0, tiled=True, axis_index_groups=same_core)
    mine = jnp.sum(slices.astype(f32), axis=0).astype(bf16)
    to_owner = []
    for a in range(arcs):
        for t in range(shards):
            z, c, y, h, odd = a // 2, a % 2, t // 4, t % 4 // 2, t % 2
            to_owner.append((a * shards + t, (2 * y + odd) * shards + (2 * y + 2 - z) % 4 * 4 + 2 * h + c))
    final = lax.ppermute(mine, ("arc", "tm"), to_owner).astype(f32)
    kind = code.astype(f32)
    carries, mirrors = kind == f32(1.0), kind == f32(2.0)
    rhs = jnp.sum(jnp.where(carries, final, f32(0.0)), axis=1)
    mirrored = jnp.sum(jnp.where(mirrors, final, f32(0.0)), axis=1, keepdims=True)
    return jnp.where(carries, jnp.concatenate([mirrored[1:], mirrored[:1]], axis=0), final), rhs


def solution(mesh):
    return jax.shard_map(
        local,
        mesh=mesh,
        in_specs=(
            P("arc", None, None, "tm"),
            P("arc", "tm", None, None),
            P("arc", None, "tm"),
            P("arc", "tm"),
            P("arc", "tm"),
        ),
        out_specs=(P(("arc", "tm"), None), P(("arc", "tm"))),
        check_vma=False,
    )
```

```python
import jax
import jax.numpy as jnp
from jax import lax
from jax.experimental import pallas as pl
from jax.experimental.pallas import tpu as pltpu
from jax.sharding import PartitionSpec as P

EP = 32
BLK = 1152
HALF = 576
SLICE = 72
ROWS = 40
TS = 16
AUG = 128
WIDE = BLK + AUG
f32 = jnp.float32
bf16 = jnp.bfloat16


def rounded(x):
    return x.astype(bf16).astype(f32)


def pack_kernel(
    cnt_ref, tr_hbm, pa_hbm, ob_hbm, f_hbm, out_ref, tr_ref, pa_ref, ob_ref, fbuf, one_ref, wt_ref, sm_ref, sems, small_sems
):
    n_blocks = fbuf.shape[2] // BLK
    smalls = [
        pltpu.make_async_copy(src, dst, small_sems.at[n])
        for n, (src, dst) in enumerate(((tr_hbm, tr_ref), (pa_hbm, pa_ref), (ob_hbm, ob_ref)))
    ]
    for copy in smalls:
        copy.start()
    middle = n_blocks // 2
    parts = [pl.ds(0, middle * BLK), pl.ds(middle * BLK, (n_blocks - middle) * BLK)]
    fetches = [pltpu.make_async_copy(f_hbm.at[:, :, p], fbuf.at[:, :, p], sems.at[n]) for n, p in enumerate(parts)]
    for copy in fetches:
        copy.start()
    lane = lax.broadcasted_iota(jnp.int32, (8, 128), 1)
    sub = lax.broadcasted_iota(jnp.int32, (8, 128), 0)
    sm_ref[...] = jnp.zeros_like(sm_ref)
    one_ref[...] = jnp.zeros_like(one_ref)
    for copy in smalls:
        copy.wait()
    for b in range(6):
        sm_ref[b : b + 1, 0:EP] = pa_ref[b]
        one_ref[b, 0:6, 0:EP] = tr_ref[b, :, 0, :]
    heads = sm_ref[...]

    def total(terms):
        return ((terms[0] + terms[1]) + (terms[2] + terms[3])) + (terms[4] + terms[5])

    def applied(maps, vectors):
        return total([maps[c] * vectors[c : c + 1, :] for c in range(6)])

    def at(maps, epoch):
        return [maps[c][:, epoch : epoch + 1] for c in range(6)]

    one = [one_ref[c] for c in range(6)]
    back = [[pltpu.roll(one[c], n, 1) for c in range(6)] for n in (1, 2, 3)]
    two = [total([one[c][m : m + 1, :] * back[0][m] for m in range(6)]) for c in range(6)]
    two_back = [pltpu.roll(two[c], 2, 1) for c in range(6)]
    four = [total([two[c][m : m + 1, :] * two_back[m] for m in range(6)]) for c in range(6)]
    heads_one = applied(back[0], heads)
    heads_two = applied(back[1], heads_one)
    heads_three = applied(back[2], heads_two)
    phase = lane & 3
    fresh = jnp.where(
        phase == 3, heads_three, jnp.where(phase == 2, heads_two, jnp.where(phase == 1, heads_one, heads))
    )
    rows = jnp.where((lane == sub + EP) & (sub < 6), f32(1.0), f32(0.0))
    for i in range(EP - 1, -1, -4):
        first = jnp.where(lane == i, heads, applied(at(one, i), rows))
        second = jnp.where(lane == i - 1, heads, jnp.where(lane == i, heads_one, applied(at(two, i), rows)))
        third = jnp.where(lane == i - 2, heads, applied(at(one, i - 2), second))
        for n, value in enumerate((rows, first, second, third)):
            wt_ref[:, i - n, :] = value[0:6, :]
        rows = jnp.where((lane >= i - 3) & (lane <= i), fresh, applied(at(four, i), rows))
    sm_ref[0:6, :] = rows[0:6, :]
    sm_ref[6:7, 0:EP] = ob_ref[...]
    lane1 = lax.broadcasted_iota(jnp.int32, (1, 128), 1)
    sm_ref[7:8, :] = jnp.where((lane1 < EP) & (lane1 < cnt_ref[0, 0]), f32(1.0), f32(0.0))
    weights = jnp.transpose(wt_ref[...].reshape(6 * EP, 128))[0:ROWS, :].astype(bf16)
    small = jnp.concatenate([sm_ref[b : b + 1, :] for b in range(8)] + [jnp.zeros((1, 128), f32)], axis=1)
    high = rounded(small)
    row = lax.broadcasted_iota(jnp.int32, (8, BLK), 0)
    tail = jnp.where(row == 6, high, jnp.where(row == 7, small - high, f32(0.0)))
    for b in range(n_blocks):
        if b % middle == 0:
            fetches[b // middle].wait()
        local = jnp.dot(weights, fbuf[:, :, b * BLK : (b + 1) * BLK].reshape(6 * EP, BLK), preferred_element_type=f32)
        packed = jnp.concatenate([local[0:EP, :], local[EP:ROWS, :] + tail], axis=0).astype(bf16)
        for h in range(2):
            out_ref[b // 2 * 4 + 2 * h + b % 2] = packed


def pack(counts, transition, partials, observed, forcing):
    n_blocks = forcing.shape[2] // BLK
    hbm = pl.BlockSpec(memory_space=pltpu.MemorySpace.HBM)
    return pl.pallas_call(
        pack_kernel,
        out_shape=jax.ShapeDtypeStruct((2 * n_blocks, ROWS, BLK), bf16),
        in_specs=[pl.BlockSpec(memory_space=pltpu.SMEM), hbm, hbm, hbm, hbm],
        out_specs=pl.BlockSpec(memory_space=pltpu.VMEM),
        scratch_shapes=[
            pltpu.VMEM((6, 6, 1, EP), f32),
            pltpu.VMEM((6, 1, EP), f32),
            pltpu.VMEM((1, EP), f32),
            pltpu.VMEM((6, EP, n_blocks * BLK), bf16),
            pltpu.VMEM((6, 8, 128), f32),
            pltpu.VMEM((6, EP, 128), f32),
            pltpu.VMEM((8, 128), f32),
            pltpu.SemaphoreType.DMA((2,)),
            pltpu.SemaphoreType.DMA((3,)),
        ],
        compiler_params=pltpu.CompilerParams(vmem_limit_bytes=32 << 20),
        name="pack_rows",
    )(counts, *[pltpu.with_memory_space_constraint(x, pltpu.MemorySpace.HBM) for x in (transition, partials, observed, forcing)])


def split(x):
    high = x.astype(bf16)
    return high, (x - high.astype(f32)).astype(bf16)


def position():
    shard = lax.axis_index("tm")
    return shard, lax.div(lax.rem(shard, 4), 2), 2 * lax.div(shard, 4) + 6 - lax.div(lax.axis_index("arc"), 2), lax.rem(lax.axis_index("arc"), 2)


def gram_slices(x_ref, l_ref, g_ref, out_ref, half, parity, turn):
    for case in range(4):

        @pl.when(2 * half + parity == case)
        def _():
            for q in range(4):
                first = 4 * SLICE * q + SLICE * case
                l_ref[:, SLICE * q : SLICE * (q + 1)] = x_ref[:, first : first + SLICE]

    g_ref[...] = lax.dot_general(
        l_ref[...], x_ref[...], (((0,), (0,)), ((), ())), preferred_element_type=f32
    ) * f32(1.0 / 4096.0)
    for q in range(4):
        at = slice(SLICE * q, SLICE * (q + 1))
        start = 4 * SLICE * q
        low, top = start // 128 * 128, min(BLK, -(-(start + 4 * SLICE) // 128) * 128)
        row = lax.broadcasted_iota(jnp.int32, (SLICE, top - low), 0)
        column = lax.broadcasted_iota(jnp.int32, (SLICE, top - low), 1) + low
        after = jnp.where(row == SLICE - 1, 0, row + 1)
        near = jnp.where(
            column == after + (start + SLICE * (2 * half + parity)), g_ref[at, BLK + 6 : BLK + 7], g_ref[at, low:top]
        )
        pieces = ([g_ref[at, 0:low]] if low else []) + [near] + ([g_ref[at, top:BLK]] if top < BLK else [])
        out_ref[lax.rem(turn + 4 - q, 4)] = jnp.concatenate(pieces, axis=1).astype(out_ref.dtype)


def normal_kernel(r_ref, send_ref, x_ref, te_ref, in_ref, lead_ref, y_ref, l_ref, g_ref):
    shard, half, turn, core = position()
    dims = (((0,), (0,)), ((), ()))
    tails = [r_ref[t, 32:40, :].astype(f32) for t in range(TS)]
    for t in range(TS):
        small = tails[t][6:7, :] + tails[t][7:8, :]
        for b in range(8):
            te_ref[8 * t + b : 8 * t + b + 1, :] = small[:, 128 * b : 128 * b + 128]
    turned = jnp.transpose(te_ref[...])

    sub = lax.broadcasted_iota(jnp.int32, (8, BLK), 0)
    sub_aug = lax.broadcasted_iota(jnp.int32, (8, AUG), 0)
    lane_aug = lax.broadcasted_iota(jnp.int32, (8, AUG), 1)
    unit = jnp.where((sub_aug == 6) & (lane_aug == 6), f32(1.0), f32(0.0))
    eye = jnp.where((lane_aug == sub_aug) & (sub_aug < 6), f32(1.0), f32(0.0))
    state = jnp.concatenate([jnp.zeros((8, BLK), f32), eye + unit], axis=1)
    for t in range(TS):
        in_ref[8 * t : 8 * t + 8, :] = state
        if t == TS - 1:
            break
        new = jnp.concatenate([jnp.where(sub < 6, tails[t], f32(0.0)), unit], axis=1)
        terms = [turned[32:40, 8 * t + b : 8 * t + b + 1] * state[b : b + 1, :] for b in range(6)]
        state = new + (((terms[0] + terms[1]) + (terms[2] + terms[3])) + (terms[4] + terms[5]))

    lane = lax.broadcasted_iota(jnp.int32, (EP, AUG), 1)
    for t in range(TS):
        active = turned[0:EP, 8 * t + 7 : 8 * t + 8] > f32(0.5)
        mine = (lane >= 8 * t) & (lane < 8 * t + 7) & active
        high, low = split(jnp.where(mine, turned[0:EP, :], f32(0.0)))
        lead_ref[EP * t : EP * t + EP, 0:AUG] = high
        lead_ref[EP * t : EP * t + EP, AUG : 2 * AUG] = low
        lead_ref[EP * t : EP * t + EP, 2 * AUG : 3 * AUG] = high

    maps = in_ref[:, BLK:WIDE]
    maps_high, maps_low = split(maps)
    states = jnp.dot(
        lead_ref[...], jnp.concatenate([maps_high, maps_high, maps_low], axis=0), preferred_element_type=f32
    )
    states_high, states_low = split(states)
    left = (states_high.astype(f32) + pltpu.roll(states_low.astype(f32), 8, 1)).astype(bf16)
    rows = jnp.concatenate([r_ref[t, 0:EP, :] for t in range(TS)], axis=0)
    from_local = lax.dot_general(left, rows, dims, preferred_element_type=f32)
    right = jnp.concatenate([states_high, states_low, lead_ref[:, 0 : 2 * AUG]], axis=1)
    from_small = lax.dot_general(left, right, dims, preferred_element_type=f32)
    from_small = from_small[0:8, :] + from_small[8:16, :]
    augmented = from_small[:, 0:AUG] + from_small[:, AUG : 2 * AUG]
    through = from_small[:, 2 * AUG : 3 * AUG] + from_small[:, 3 * AUG : 4 * AUG]
    through_high, through_low = split(through)
    sums_high, sums_low = split(in_ref[:, 0:BLK])
    from_sums = jnp.dot(
        jnp.concatenate([through_high, through_low, through_high], axis=1),
        jnp.concatenate([sums_high, sums_high, sums_low], axis=0),
        preferred_element_type=f32,
    )
    system = jnp.concatenate([from_local[0:8, :] + from_local[8:16, :] + from_sums, augmented + eye], axis=1)
    row_id = lax.broadcasted_iota(jnp.int32, (8, WIDE), 0)
    for p in range(6):
        column = system[:, BLK + p : BLK + p + 1]
        pivot = system[p : p + 1, :] * (f32(1.0) / system[p : p + 1, BLK + p : BLK + p + 1])
        system = jnp.where(row_id == p, pivot, system - column * pivot)

    for t in range(TS):
        at = slice(8 * t, 8 * t + 8)
        terms = [in_ref[at, BLK + c : BLK + c + 1] * system[c : c + 1, :] for c in range(6)]
        in_ref[at, :] = in_ref[at, :] - (((terms[0] + terms[1]) + (terms[2] + terms[3])) + (terms[4] + terms[5]))
    change_high, change_low = split(in_ref[...])
    y_ref[...] = jnp.dot(
        lead_ref[...], jnp.concatenate([change_high, change_high, change_low], axis=0), preferred_element_type=f32
    )
    lane_tail = lax.broadcasted_iota(jnp.int32, (EP, AUG), 1)
    for t in range(TS):
        at = slice(EP * t, EP * t + EP)
        active = turned[0:EP, 8 * t + 7 : 8 * t + 8] > f32(0.5)
        local = jnp.where(active, r_ref[t, 0:EP, :].astype(f32), f32(0.0))
        x_ref[at, 0:BLK] = (local + y_ref[at, 0:BLK]).astype(bf16)
        x_ref[at, BLK:WIDE] = jnp.where(lane_tail == 6, y_ref[at, BLK:WIDE], f32(0.0)).astype(bf16)

    gram_slices(x_ref, l_ref, g_ref, send_ref, half, 1 - core, turn)


def own_kernel(x_ref, keep_ref, code_ref, l_ref, g_ref):
    shard, half, turn, core = position()
    gram_slices(x_ref, l_ref, g_ref, keep_ref, half, core, turn)
    row = lax.broadcasted_iota(jnp.int32, (SLICE, BLK), 0)
    column = lax.broadcasted_iota(jnp.int32, (SLICE, BLK), 1) - SLICE * shard
    carries = column == jnp.where(row == SLICE - 1, 0, row + 1)
    mirrors = column == jnp.where(row == 0, SLICE - 1, row - 1)
    code_ref[...] = jnp.where(carries, f32(1.0), jnp.where(mirrors, f32(2.0), f32(0.0))).astype(bf16)


def normals(received):
    vmem = pl.BlockSpec(memory_space=pltpu.VMEM)
    return pl.pallas_call(
        normal_kernel,
        out_shape=(jax.ShapeDtypeStruct((4, SLICE, BLK), bf16), jax.ShapeDtypeStruct((TS * EP, WIDE), bf16)),
        in_specs=[vmem],
        out_specs=(vmem, vmem),
        scratch_shapes=[
            pltpu.VMEM((8 * TS, 128), f32),
            pltpu.VMEM((8 * TS, WIDE), f32),
            pltpu.VMEM((TS * EP, 3 * AUG), bf16),
            pltpu.VMEM((TS * EP, WIDE), f32),
            pltpu.VMEM((TS * EP, HALF // 2), bf16),
            pltpu.VMEM((HALF // 2, WIDE), f32),
        ],
        compiler_params=pltpu.CompilerParams(vmem_limit_bytes=32 << 20),
        name="normal_rows",
    )(received)


def own_slices(rows):
    vmem = pl.BlockSpec(memory_space=pltpu.VMEM)
    return pl.pallas_call(
        own_kernel,
        out_shape=(jax.ShapeDtypeStruct((4, SLICE, BLK), f32), jax.ShapeDtypeStruct((SLICE, BLK), bf16)),
        in_specs=[vmem],
        out_specs=(vmem, vmem),
        scratch_shapes=[pltpu.VMEM((TS * EP, HALF // 2), bf16), pltpu.VMEM((HALF // 2, WIDE), f32)],
        cost_estimate=pl.CostEstimate(flops=2 * TS * EP * WIDE * HALF // 2, bytes_accessed=4 << 20, transcendentals=0),
        compiler_params=pltpu.CompilerParams(vmem_limit_bytes=24 << 20),
        name="own_slices",
    )(rows)


def local(transition, forcing, partials, observed, counts):
    packed = pack(
        counts,
        jnp.transpose(transition, (1, 2, 0, 3)),
        jnp.transpose(partials, (1, 0, 2)),
        observed,
        jnp.transpose(forcing[0], (1, 0, 2)),
    )
    received = lax.all_to_all(packed, "tm", split_axis=0, concat_axis=0, tiled=True)
    send, rows = normals(received)
    arcs, shards = lax.axis_size("arc"), lax.axis_size("tm")
    other_core = [(a * shards + t, (a ^ 1) * shards + t) for a in range(arcs) for t in range(shards)]
    arrived = lax.ppermute(send, ("arc", "tm"), other_core)
    keep, code = own_slices(rows)
    final = None
    for k in range(3, -1, -1):
        pair_sum = (keep[k] + arrived[k].astype(f32)).astype(bf16)
        to_owner = []
        for a in range(arcs):
            for t in range(shards):
                z, c, y, h, odd = a // 2, a % 2, t // 4, t % 4 // 2, t % 2
                to_owner.append((a * shards + t, (2 * y + odd) * shards + (2 * y + 2 - z - k) % 4 * 4 + 2 * h + c))
        part = lax.ppermute(pair_sum, ("arc", "tm"), to_owner).astype(f32)
        final = part if final is None else final + part
    kind = code.astype(f32)
    carries, mirrors = kind == f32(1.0), kind == f32(2.0)
    rhs = jnp.sum(jnp.where(carries, final, f32(0.0)), axis=1)
    mirrored = jnp.sum(jnp.where(mirrors, final, f32(0.0)), axis=1, keepdims=True)
    return jnp.where(carries, jnp.concatenate([mirrored[1:], mirrored[:1]], axis=0), final), rhs


def solution(mesh):
    return jax.shard_map(
        local,
        mesh=mesh,
        in_specs=(
            P("arc", None, None, "tm"),
            P("arc", "tm", None, None),
            P("arc", None, "tm"),
            P("arc", "tm"),
            P("arc", "tm"),
        ),
        out_specs=(P(("arc", "tm"), None), P(("arc", "tm"))),
        check_vma=False,
    )
```
